512 devices in a mesh: section: 16 (over y, x_lo, core), dp: 32 (over x_hi, z).
Axes of the slice: x: 4 (x_hi: 2, x_lo: 2; x = x_hi * 2 + x_lo), y: 4, z: 16, core: 2. Of those that a mesh axis runs over, the one named last changes fastest.
Arguments:
- acts: bfloat16 [16, 2, 4096, 512], P('section', None, 'dp'), may hold values from -12 to 12
- weights: bfloat16 [16, 512, 512], P('section'), may hold values from -0.25 to 0.25
- cot_last: bfloat16 [2, 4096, 512], P(None, 'dp'), may hold values from -1.796875 to 1.796875
Outputs:
- input_cots: bfloat16 [16, 2, 4096, 512], P('section', None, 'dp')
- update: float32 [16, 512, 512], P('section')
The draws below stay inside these ranges and needn't reach their ends.
All inputs are finite; a program needn't handle non-finite values.
Results may differ from the reference program's by a relative error of at most 0.025.
Values may be sent and summed in bfloat16 or wider, within the bound.
A program may use at most 64 MiB of HBM per device.

```python
import jax
import jax.numpy as jnp
from jax import lax

BLK = 512
MB = 2
NS_STEPS = 3
SECTIONS = 16
TOKENS = 4096


def draw_acts(key, part):
    first, second = jax.random.split(key, 2)
    scales = jnp.exp(jax.random.uniform(first, (SECTIONS, 1, 1, BLK), jnp.float32, jnp.log(0.3), jnp.log(3.0)))
    base = jax.random.normal(second, (SECTIONS, MB, TOKENS, BLK), jnp.float32)
    base = jnp.clip(base, -4.0, 4.0)
    return (base * scales).astype(jnp.bfloat16)


def shard_levels(key, extent, pieces, smallest, top_value):
    level, own = 1.0, jax.random.fold_in(key, 6)
    for dim, blocks in pieces:
        draws = jnp.exp(jax.random.uniform(jax.random.fold_in(own, dim), (blocks,), jnp.float32, smallest / len(pieces), top_value / len(pieces)))
        level = level * jnp.repeat(draws, extent[dim] // blocks).reshape([-1 if axis == dim else 1 for axis in range(len(extent))])
    return level


def scatter_about(stream_key, dims, scale, limit, pieces=(), kind=jnp.bfloat16):
    drawn = scale * jax.random.normal(stream_key, dims, jnp.float32)
    if pieces:
        drawn = drawn * shard_levels(stream_key, dims, pieces, -0.22, 0.18)
    return jnp.clip(drawn, -limit, limit).astype(kind)


def setup_inputs(seed: int = 0) -> dict:
    streams_of = jax.random.split(jax.random.key(seed), 4)
    return {
        "acts": draw_acts(jax.random.fold_in(streams_of[3], 71), 0),
        "weights": scatter_about(streams_of[1], (SECTIONS, BLK, BLK), BLK ** -0.5, 0.25, ((0, 16),)),
        "cot_last": scatter_about(streams_of[2], (MB, TOKENS, BLK), 0.3, 1.796875, ((1, 32),)),
    }


def silu_slope(pre):
    sig = jax.nn.sigmoid(pre)
    return sig * (1.0 + pre * (1.0 - sig))

def moment(left, right):
    return lax.dot_general(left, right, (((0,), (0,)), ((), ())), preferred_element_type=jnp.float32)

def newton(matrix):
    eye = jnp.eye(matrix.shape[0], dtype=jnp.float32)
    approx = eye / jnp.sqrt(jnp.sum(matrix * matrix))
    for step in range(NS_STEPS):
        inner = jnp.dot(matrix, approx, precision=lax.Precision.HIGHEST)
        approx = 2.0 * approx - jnp.dot(approx, inner, precision=lax.Precision.HIGHEST)
    return approx

def reference(acts, weights, cot_last):
    count = MB * TOKENS
    eye = jnp.eye(BLK, dtype=jnp.float32)
    upstream = cot_last.reshape(MB * TOKENS, BLK)
    cots = [None] * SECTIONS
    updates = [None] * SECTIONS
    for section in range(SECTIONS - 1, -1, -1):
        inputs = acts[section].reshape(MB * TOKENS, BLK)
        weight = weights[section]
        pre = jnp.dot(inputs, weight, preferred_element_type=jnp.float32)
        slope_dh = (upstream.astype(jnp.float32) * silu_slope(pre)).astype(jnp.bfloat16)
        back = lax.dot_general(slope_dh, weight, (((1,), (1,)), ((), ())), preferred_element_type=jnp.float32)
        result = (upstream.astype(jnp.float32) + back).astype(jnp.bfloat16)
        cots[section] = result.reshape(MB, TOKENS, BLK)
        act_factor = moment(inputs, inputs) / count + 0.01 * eye
        out_factor = moment(slope_dh, slope_dh) / count + 0.01 * eye
        grad = moment(inputs, slope_dh)
        act_inv = newton(act_factor)
        out_inv = newton(out_factor)
        updates[section] = jnp.dot(jnp.dot(act_inv, grad, precision=lax.Precision.HIGHEST), out_inv, precision=lax.Precision.HIGHEST)
        upstream = result
    return (jnp.stack(cots), jnp.stack(updates))
```

```python
import functools

import jax
import jax.numpy as jnp
from jax import lax
from jax.experimental import pallas as pl
from jax.experimental.pallas import tpu as pltpu
from jax.sharding import PartitionSpec as P

MESH = pl.DeviceIdType.MESH
T = 128
SUB = 2


def dot(a, b):
    return jnp.dot(a, b, preferred_element_type=jnp.float32)


def kernel(
    sections, rings, size,
    acts_ref, w_ref, cot_ref, dx_ref, up_ref,
    slope, xt, dyin, dh, own, stage, rbuf, red, xs, xr, full, tb, ub, zb,
    c_send, c_recv, r_send, r_recv, x_sem, g_send, g_recv,
):
    s = lax.axis_index("section")
    p = lax.axis_index("dp")
    z, ring = lax.rem(p, size), p // size
    base = ring * size
    up = (s, base + lax.rem(z + 1, size))
    down = (s, base + lax.rem(z + size - 1, size))
    over = (s, lax.rem(p + size, rings * size))
    width = w_ref.shape[1]
    nb = width // T
    half = size // 2
    piece = own.shape[0] // size
    sub = piece // SUB
    micro, rows = acts_ref.shape[1], acts_ref.shape[2]
    count = micro * rows * rings * size

    barrier = pltpu.get_barrier_semaphore()
    for peer in (up, down, over, (lax.rem(s + 1, sections), p)):
        pl.semaphore_signal(barrier, inc=1, device_id=peer, device_id_type=MESH)

    for m in range(micro):
        pre = dot(acts_ref[0, m], w_ref[0])
        sig = 1.0 / (1.0 + jnp.exp(-pre))
        slope[m] = sig * (1.0 + pre * (1.0 - sig))

    def prepare():
        x = acts_ref[0].reshape(micro * rows, width)
        xt[...] = x.T
        at = 0
        for i in range(nb):
            prod = dot(xt[i * T:(i + 1) * T, :], x[:, i * T:])
            for j in range(nb - i):
                own[pl.ds((at + j) * T, T), :] = prod[:, j * T:(j + 1) * T]
            at += nb - i

    @pl.when(s < sections - 1)
    def _():
        prepare()

    pl.semaphore_wait(barrier, 4)

    def chain_copy(m):
        return pltpu.make_async_remote_copy(
            src_ref=dx_ref.at[0, m], dst_ref=dyin.at[m],
            send_sem=c_send.at[m], recv_sem=c_recv.at[m],
            device_id=(s - 1, p), device_id_type=MESH,
        )

    @pl.when(s == sections - 1)
    def _():
        dyin[...] = cot_ref[...]

    for m in range(micro):
        @pl.when(s < sections - 1)
        def _():
            chain_copy(m).wait_recv()
        dy = dyin[m].astype(jnp.float32)
        part = (dy * slope[m]).astype(jnp.bfloat16)
        dh[m * rows:(m + 1) * rows, :] = part
        back = lax.dot_general(
            part, w_ref[0], (((1,), (1,)), ((), ())), preferred_element_type=jnp.float32
        )
        dx_ref[0, m] = (dy + back).astype(jnp.bfloat16)

        @pl.when(s > 0)
        def _():
            chain_copy(m).start()

    @pl.when(s == sections - 1)
    def _():
        prepare()

    ntri = nb * (nb + 1) // 2
    d = dh[...]
    dt = d.T
    at = ntri
    for i in range(nb):
        prod = dot(dt[i * T:(i + 1) * T, :], d[:, i * T:])
        for j in range(nb - i):
            own[pl.ds((at + j) * T, T), :] = prod[:, j * T:(j + 1) * T]
        at += nb - i
    for i in range(nb):
        prod = dot(xt[i * T:(i + 1) * T, :], d)
        for j in range(nb):
            own[pl.ds((at + j) * T, T), :] = prod[:, j * T:(j + 1) * T]
        at += nb

    def rows_of(chunk, k):
        return pl.ds(pl.multiple_of(chunk * piece + k * sub, 16), sub)

    def ring_copy(way, t, k):
        return pltpu.make_async_remote_copy(
            src_ref=stage.at[way, t, k], dst_ref=rbuf.at[way, t, k],
            send_sem=r_send.at[way, t, k], recv_sem=r_recv.at[way, t, k],
            device_id=(up, down)[way], device_id_type=MESH,
        )

    def ring_send(way, t, k, first):
        chunk = lax.rem(z + half - t if way == 0 else z + half + t, size)
        value = own[rows_of(chunk, k), :]
        if not first:
            ring_copy(way, t - 1, k).wait_recv()
            value = value + rbuf[way, t - 1, k].astype(jnp.float32)
        stage[way, t, k] = value.astype(jnp.bfloat16)
        ring_copy(way, t, k).start()

    for k in range(SUB):
        ring_send(0, 0, k, True)
        ring_send(1, 1, k, True)
    for k in range(SUB):
        ring_send(0, 1, k, False)

    def ring_step(t, carry):
        for k in range(SUB):
            for way in range(2):
                ring_send(way, t, k, False)
        return carry

    lax.fori_loop(2, half, ring_step, 0)

    def over_copy(k):
        return pltpu.make_async_remote_copy(
            src_ref=xs.at[k], dst_ref=xr.at[k], send_sem=x_sem.at[0, k],
            recv_sem=x_sem.at[1, k], device_id=over, device_id_type=MESH,
        )

    for k in range(SUB):
        value = own[rows_of(z, k), :]
        for way in range(2):
            ring_copy(way, half - 1, k).wait_recv()
            value = value + rbuf[way, half - 1, k].astype(jnp.float32)
        xs[k] = value.astype(jnp.bfloat16)
        over_copy(k).start()

    def gather_copy(way, t, k):
        chunk = lax.rem(z + size - t if way == 0 else z + t, size)
        return pltpu.make_async_remote_copy(
            src_ref=red.at[rows_of(chunk, k), :], dst_ref=red.at[rows_of(chunk, k), :],
            send_sem=g_send.at[way, t, k], recv_sem=g_recv.at[way, t, k],
            device_id=(up, down)[way], device_id_type=MESH,
        )

    def arrived(way, t, k):
        chunk = lax.rem(z + 2 * size - 1 - t if way == 0 else z + 1 + t, size)
        return pltpu.make_async_remote_copy(
            src_ref=red.at[rows_of(chunk, k), :], dst_ref=red.at[rows_of(chunk, k), :],
            send_sem=g_send.at[way, t, k], recv_sem=g_recv.at[way, t, k],
            device_id=(up, down)[way], device_id_type=MESH,
        )

    for k in range(SUB):
        over_copy(k).wait_recv()
        total = xs[k].astype(jnp.float32) + xr[k].astype(jnp.float32)
        red[rows_of(z, k), :] = total.astype(jnp.bfloat16)
        for way in range(2):
            gather_copy(way, 0, k).start()

    def gather_step(t, carry):
        for k in range(SUB):
            for way in range(2):
                arrived(way, t - 1, k).wait_recv()
                gather_copy(way, t, k).start()
        return carry

    lax.fori_loop(1, half - 1, gather_step, 0)
    for k in range(SUB):
        arrived(0, half - 2, k).wait_recv()
        gather_copy(0, half - 1, k).start()
    for k in range(SUB):
        arrived(1, half - 2, k).wait_recv()
        arrived(0, half - 1, k).wait_recv()

    def unpack(at, side):
        for i in range(nb):
            for j in range(i, nb):
                block = red[pl.ds(at * T, T), :].astype(jnp.float32) / count
                if i == j:
                    row = lax.broadcasted_iota(jnp.int32, (T, T), 0)
                    col = lax.broadcasted_iota(jnp.int32, (T, T), 1)
                    block = block + jnp.where(row == col, 0.01, 0.0)
                    full[i * T:(i + 1) * T, j * T:(j + 1) * T] = block
                else:
                    full[i * T:(i + 1) * T, j * T:(j + 1) * T] = block
                    full[j * T:(j + 1) * T, i * T:(i + 1) * T] = block.T
                at += 1
        m = full[...]
        inv = 1.0 / jnp.sqrt(jnp.sum(m * m, keepdims=True))
        tb[0] = (m * inv).astype(jnp.bfloat16)
        for h in range(2):
            r = slice(h * (width // 2), (h + 1) * (width // 2))
            t = full[r, :] * inv
            ub[0, r, :] = 2.0 * t - dot(tb[0, r, :], tb[0])
        tb[1] = ub[0].astype(jnp.bfloat16)
        for h in range(2):
            r = slice(h * (width // 2), (h + 1) * (width // 2))
            u = ub[0, r, :]
            ub[1, r, :] = 2.0 * u - dot(tb[1, r, :], tb[1])
        tb[2] = ub[1].astype(jnp.bfloat16)
        for h in range(2):
            r = slice(h * (width // 2), (h + 1) * (width // 2))
            y = 2.0 * (full[r, :] * inv + ub[0, r, :]) - dot(tb[0, r, :], tb[1])
            zz = 4.0 * ub[1, r, :] + 2.0 * y - dot(y.astype(jnp.bfloat16), tb[2])
            zb[side, r, :] = zz.astype(jnp.bfloat16)
        return inv

    inv_a = unpack(0, 0)
    inv_o = unpack(ntri, 1)
    for i in range(nb):
        for j in range(nb):
            block = red[pl.ds((2 * ntri + i * nb + j) * T, T), :]
            tb[0, i * T:(i + 1) * T, j * T:(j + 1) * T] = block
    scale = inv_a * inv_o
    for h in range(2):
        r = slice(h * (width // 2), (h + 1) * (width // 2))
        full[r, :] = 8.0 * tb[0, r, :].astype(jnp.float32) - dot(tb[0, r, :], zb[1])
    tb[1] = full[...].astype(jnp.bfloat16)
    for h in range(2):
        r = slice(h * (width // 2), (h + 1) * (width // 2))
        up_ref[0, r, :] = (8.0 * full[r, :] - dot(zb[0, r, :], tb[1])) * scale

    @pl.when(s > 0)
    def _():
        for m in range(micro):
            chain_copy(m).wait_send()

    def drain(t, carry):
        for k in range(SUB):
            ring_copy(0, t, k).wait_send()
            gather_copy(0, t, k).wait_send()
        return carry

    lax.fori_loop(0, half, drain, 0)

    def drain_down(t, carry):
        for k in range(SUB):
            ring_copy(1, t + 1, k).wait_send()
            gather_copy(1, t, k).wait_send()
        return carry

    lax.fori_loop(0, half - 1, drain_down, 0)
    for k in range(SUB):
        over_copy(k).wait_send()


def body(rings, acts, weights, cot_last):
    sections = lax.axis_size("section")
    size = lax.axis_size("dp") // rings
    _, micro, rows, width = acts.shape
    nb = width // T
    total = (nb * (nb + 1) + nb * nb) * T
    piece = total // size
    half = size // 2
    vmem = pl.BlockSpec(memory_space=pltpu.VMEM)
    bf16, f32 = jnp.bfloat16, jnp.float32
    dma = pltpu.SemaphoreType.DMA
    return pl.pallas_call(
        functools.partial(kernel, sections, rings, size),
        name="relay",
        out_shape=(
            jax.ShapeDtypeStruct((1, micro, rows, width), bf16),
            jax.ShapeDtypeStruct((1, width, width), f32),
        ),
        in_specs=[vmem] * 3,
        out_specs=(vmem, vmem),
        scratch_shapes=[
            pltpu.VMEM((micro, rows, width), f32),
            pltpu.VMEM((width, micro * rows), bf16),
            pltpu.VMEM((micro, rows, width), bf16),
            pltpu.VMEM((micro * rows, width), bf16),
            pltpu.VMEM((total, T), f32),
            pltpu.VMEM((2, half, SUB, piece // SUB, T), bf16),
            pltpu.VMEM((2, half, SUB, piece // SUB, T), bf16),
            pltpu.VMEM((total, T), bf16),
            pltpu.VMEM((SUB, piece // SUB, T), bf16),
            pltpu.VMEM((SUB, piece // SUB, T), bf16),
            pltpu.VMEM((width, width), f32),
            pltpu.VMEM((3, width, width), bf16),
            pltpu.VMEM((2, width, width), f32),
            pltpu.VMEM((2, width, width), bf16),
            dma((micro,)), dma((micro,)),
            dma((2, half, SUB)), dma((2, half, SUB)),
            dma((2, SUB)),
            dma((2, half, SUB)), dma((2, half, SUB)),
        ],
        compiler_params=pltpu.CompilerParams(
            collective_id=0, has_side_effects=True, vmem_limit_bytes=40 << 20
        ),
    )(acts, weights, cot_last)


def solution(mesh):
    placed = (P("section", None, "dp", None), P("section", None, None), P(None, "dp", None))
    return jax.shard_map(
        functools.partial(body, 2),
        mesh=mesh,
        in_specs=placed,
        out_specs=(P("section", None, "dp", None), P("section", None, None)),
        check_vma=False,
    )
```

```python
import functools

import jax
import jax.numpy as jnp
from jax import lax
from jax.experimental import pallas as pl
from jax.experimental.pallas import tpu as pltpu
from jax.sharding import PartitionSpec as P

MESH = pl.DeviceIdType.MESH
T = 128
ROWS = 32


def dot(a, b):
    return jnp.dot(a, b, preferred_element_type=jnp.float32)


def pieces_of(width, size):
    nb = width // T
    tri, square = nb * (nb + 1) // 2 * T, nb * nb * T
    o, g = tri // size, square // size // 2
    return ((o, 0, 0, o), (g, o, tri, 2 * g), (g, o + g, tri + g, 2 * g))


def kernel(
    sections, rings, size,
    acts_hbm, w_hbm, cot_hbm, dx_ref, up_ref,
    x_ref, w_ref, slope, xt, dyin, dh, own, stage, rbuf, red, xs, xr,
    astage, abuf, ared, axs, axr, full, tb, ub, zb,
    in_sem, c_send, c_recv, r_send, r_recv, x_sem, g_send, g_recv,
    a_send, a_recv, b_send, b_recv, ax_sem,
):
    s = lax.axis_index("section")
    p = lax.axis_index("dp")
    z, ring = lax.rem(p, size), p // size
    base = ring * size
    up = (s, base + lax.rem(z + 1, size))
    down = (s, base + lax.rem(z + size - 1, size))
    over = (s, lax.rem(p + size, rings * size))
    width = w_ref.shape[1]
    nb = width // T
    tri = nb * (nb + 1) // 2 * T
    half = size // 2
    pieces = pieces_of(width, size)
    each = range(len(pieces))
    micro, rows = dyin.shape[0], dyin.shape[1]
    per = rows // ROWS
    count = micro * rows * rings * size
    apiece = tri // size
    f32, bf16 = jnp.float32, jnp.bfloat16

    barrier = pltpu.get_barrier_semaphore()
    for peer in (over, (lax.rem(s + 1, sections), p)):
        pl.semaphore_signal(barrier, inc=1, device_id=peer, device_id_type=MESH)

    def greet(d, carry):
        peer = (s, base + lax.rem(z + d, size))
        pl.semaphore_signal(barrier, inc=1, device_id=peer, device_id_type=MESH)
        return carry

    lax.fori_loop(1, size, greet, 0)

    get_x = pltpu.make_async_copy(acts_hbm.at[0], x_ref, in_sem.at[0])
    get_w = pltpu.make_async_copy(w_hbm.at[0], w_ref, in_sem.at[1])
    get_c = pltpu.make_async_copy(cot_hbm, dyin, in_sem.at[2])
    get_x.start()
    get_w.start()

    @pl.when(s == sections - 1)
    def _():
        get_c.start()

    get_x.wait()
    get_w.wait()

    for m in range(micro):
        pre = dot(x_ref[m], w_ref[...])
        sig = 1.0 / (1.0 + jnp.exp(-pre))
        slope[m] = sig * (1.0 + pre * (1.0 - sig))

    pl.semaphore_wait(barrier, size + 1)

    def a_copy(d):
        chunk = lax.rem(z + d, size)
        return pltpu.make_async_remote_copy(
            src_ref=astage.at[pl.ds(pl.multiple_of(chunk * apiece, 16), apiece), :],
            dst_ref=abuf.at[d], send_sem=a_send.at[d], recv_sem=a_recv.at[d],
            device_id=(s, base + chunk), device_id_type=MESH,
        )

    def b_copy(d):
        mine = ared.at[pl.ds(pl.multiple_of(z * apiece, 16), apiece), :]
        return pltpu.make_async_remote_copy(
            src_ref=mine, dst_ref=mine, send_sem=b_send.at[d], recv_sem=b_recv.at[d],
            device_id=(s, base + lax.rem(z + d, size)), device_id_type=MESH,
        )

    def b_arrived(d):
        chunk = lax.rem(z + size - d, size)
        mine = ared.at[pl.ds(pl.multiple_of(chunk * apiece, 16), apiece), :]
        return pltpu.make_async_remote_copy(
            src_ref=mine, dst_ref=mine, send_sem=b_send.at[d], recv_sem=b_recv.at[d],
            device_id=(s, base + chunk), device_id_type=MESH,
        )

    ax_copy = pltpu.make_async_remote_copy(
        src_ref=axs, dst_ref=axr, send_sem=ax_sem.at[0], recv_sem=ax_sem.at[1],
        device_id=over, device_id_type=MESH,
    )

    def both_ways(start):
        def step(i, carry):
            start(i)
            start(size - i)
            return carry

        lax.fori_loop(1, half, step, 0)
        start(half)

    def a_start():
        x = x_ref[...].reshape(micro * rows, width)
        xt[...] = x.T
        at = 0
        for i in range(nb):
            prod = dot(xt[i * T:(i + 1) * T, :], x[:, i * T:]).astype(bf16)
            for j in range(nb - i):
                astage[(at + j) * T:(at + j + 1) * T, :] = prod[:, j * T:(j + 1) * T]
            at += nb - i
        both_ways(lambda d: a_copy(d).start())

    def a_middle():
        def add(d, total):
            a_copy(d).wait_recv()
            return total + abuf[d].astype(f32)

        first = astage[pl.ds(pl.multiple_of(z * apiece, 16), apiece), :].astype(f32)
        axs[...] = lax.fori_loop(1, size, add, first).astype(bf16)
        ax_copy.start()
        ax_copy.wait_recv()
        total = axs[...].astype(f32) + axr[...].astype(f32)
        ared[pl.ds(pl.multiple_of(z * apiece, 16), apiece), :] = total.astype(bf16)
        both_ways(lambda d: b_copy(d).start())

    @pl.when(s < sections - 2)
    def _():
        a_start()

    @pl.when(s < sections // 2)
    def _():
        a_middle()

    def chain_copy(m, r):
        return pltpu.make_async_remote_copy(
            src_ref=dx_ref.at[0, m, pl.ds(r * ROWS, ROWS), :],
            dst_ref=dyin.at[m, pl.ds(r * ROWS, ROWS), :],
            send_sem=c_send.at[m, r], recv_sem=c_recv.at[m, r],
            device_id=(s - 1, p), device_id_type=MESH,
        )

    @pl.when(s == sections - 1)
    def _():
        get_c.wait()

    def relay(step, carry):
        m, r = step // per, lax.rem(step, per)

        @pl.when(s < sections - 1)
        def _():
            chain_copy(m, r).wait_recv()

        at = pl.ds(pl.multiple_of(r * ROWS, ROWS), ROWS)
        dy = dyin[m, at, :].astype(f32)
        part = (dy * slope[m, at, :]).astype(bf16)
        dh[pl.ds(pl.multiple_of(step * ROWS, ROWS), ROWS), :] = part
        back = lax.dot_general(
            part, w_ref[...], (((1,), (1,)), ((), ())), preferred_element_type=f32
        )
        dx_ref[0, m, at, :] = (dy + back).astype(bf16)

        @pl.when(s > 0)
        def _():
            chain_copy(m, r).start()

        return carry

    lax.fori_loop(0, micro * per, relay, 0)

    @pl.when(s >= sections - 2)
    def _():
        a_start()

    d = dh[...]
    dt = d.T
    at = 0
    for i in range(nb):
        prod = dot(dt[i * T:(i + 1) * T, :], d[:, i * T:])
        for j in range(nb - i):
            own[(at + j) * T:(at + j + 1) * T, :] = prod[:, j * T:(j + 1) * T]
        at += nb - i
    for i in range(nb):
        prod = dot(xt[i * T:(i + 1) * T, :], d)
        for j in range(nb):
            own[(at + j) * T:(at + j + 1) * T, :] = prod[:, j * T:(j + 1) * T]
        at += nb

    @pl.when(s >= sections // 2)
    def _():
        a_middle()

    def rows_of(chunk, k):
        n, _, first, stride = pieces[k]
        return pl.ds(pl.multiple_of(first + chunk * stride, 16), n)

    def part_of(k):
        n, first, _, _ = pieces[k]
        return slice(first, first + n)

    def slot(k):
        n, first, _, _ = pieces[k]
        return pl.ds(first, n)

    def ring_copy(way, t, k):
        return pltpu.make_async_remote_copy(
            src_ref=stage.at[way, t, slot(k), :], dst_ref=rbuf.at[way, t, slot(k), :],
            send_sem=r_send.at[way, t, k], recv_sem=r_recv.at[way, t, k],
            device_id=(up, down)[way], device_id_type=MESH,
        )

    def ring_send(way, t, k, first):
        chunk = lax.rem(z + half - t if way == 0 else z + half + t, size)
        value = own[rows_of(chunk, k), :]
        if not first:
            ring_copy(way, t - 1, k).wait_recv()
            value = value + rbuf[way, t - 1, part_of(k), :].astype(f32)
        stage[way, t, part_of(k), :] = value.astype(bf16)
        ring_copy(way, t, k).start()

    for k in each:
        ring_send(0, 0, k, True)
        ring_send(1, 1, k, True)
    for k in each:
        ring_send(0, 1, k, False)

    def ring_step(t, carry):
        for k in each:
            for way in range(2):
                ring_send(way, t, k, False)
        return carry

    halves = [slice(h * (width // 2), (h + 1) * (width // 2)) for h in range(2)]

    def newton_first(src):
        at = 0
        for i in range(nb):
            for j in range(i, nb):
                block = src[at * T:(at + 1) * T, :].astype(f32) / count
                if i == j:
                    row = lax.broadcasted_iota(jnp.int32, (T, T), 0)
                    col = lax.broadcasted_iota(jnp.int32, (T, T), 1)
                    block = block + jnp.where(row == col, 0.01, 0.0)
                else:
                    full[j * T:(j + 1) * T, i * T:(i + 1) * T] = block.T
                full[i * T:(i + 1) * T, j * T:(j + 1) * T] = block
                at += 1
        m = full[...]
        inv = 1.0 / jnp.sqrt(jnp.sum(m * m, keepdims=True))
        t = m * inv
        full[...] = t
        tb[0] = t.astype(bf16)
        return inv

    def newton_second():
        for r in halves:
            u = 2.0 * full[r, :] - dot(tb[0, r, :], tb[0])
            ub[0, r, :] = u
            tb[1, r, :] = u.astype(bf16)

    def newton_third():
        for r in halves:
            v = 2.0 * ub[0, r, :] - dot(tb[1, r, :], tb[1])
            ub[1, r, :] = v
            tb[2, r, :] = v.astype(bf16)

    def newton_last(side):
        for r in halves:
            y = 2.0 * (full[r, :] + ub[0, r, :]) - dot(tb[0, r, :], tb[1])
            last = 4.0 * ub[1, r, :] + 2.0 * y - dot(y.astype(bf16), tb[2])
            zb[side, r, :] = last.astype(bf16)

    lax.fori_loop(2, half - 3, ring_step, 0)

    def a_wait(d, carry):
        b_arrived(d).wait_recv()
        return carry

    lax.fori_loop(1, size, a_wait, 0)
    inv_a = newton_first(ared)
    ring_step(half - 3, 0)
    newton_second()
    ring_step(half - 2, 0)
    newton_third()
    ring_step(half - 1, 0)
    newton_last(0)

    def over_copy(k):
        return pltpu.make_async_remote_copy(
            src_ref=xs.at[slot(k), :], dst_ref=xr.at[slot(k), :], send_sem=x_sem.at[0, k],
            recv_sem=x_sem.at[1, k], device_id=over, device_id_type=MESH,
        )

    for k in each:
        value = own[rows_of(z, k), :]
        for way in range(2):
            ring_copy(way, half - 1, k).wait_recv()
            value = value + rbuf[way, half - 1, part_of(k), :].astype(f32)
        xs[part_of(k), :] = value.astype(bf16)
        over_copy(k).start()

    def gather_copy(way, t, k, chunk):
        there = red.at[rows_of(chunk, k), :]
        return pltpu.make_async_remote_copy(
            src_ref=there, dst_ref=there,
            send_sem=g_send.at[way, t, k], recv_sem=g_recv.at[way, t, k],
            device_id=(up, down)[way], device_id_type=MESH,
        )

    def pass_on(way, t, k):
        return gather_copy(way, t, k, lax.rem(z + size - t if way == 0 else z + t, size))

    def arrived(way, t, k):
        return gather_copy(
            way, t, k, lax.rem(z + 2 * size - 1 - t if way == 0 else z + 1 + t, size)
        )

    for k in each:
        over_copy(k).wait_recv()
        total = xs[part_of(k), :].astype(f32) + xr[part_of(k), :].astype(f32)
        red[rows_of(z, k), :] = total.astype(bf16)
        for way in range(2):
            pass_on(way, 0, k).start()

    def gather_step(t, carry):
        for k in each:
            for way in range(2):
                arrived(way, t - 1, k).wait_recv()
                pass_on(way, t, k).start()
        return carry

    lax.fori_loop(1, half - 1, gather_step, 0)
    for k in each:
        arrived(0, half - 2, k).wait_recv()
        pass_on(0, half - 1, k).start()
    arrived(1, half - 2, 0).wait_recv()
    arrived(0, half - 1, 0).wait_recv()

    inv_o = newton_first(red)
    newton_second()
    newton_third()
    newton_last(1)
    for k in each[1:]:
        arrived(1, half - 2, k).wait_recv()
        arrived(0, half - 1, k).wait_recv()
    for i in range(nb):
        for j in range(nb):
            block = red[tri + (i * nb + j) * T:tri + (i * nb + j + 1) * T, :]
            tb[0, i * T:(i + 1) * T, j * T:(j + 1) * T] = block
    scale = inv_a * inv_o
    for r in halves:
        h = 8.0 * tb[0, r, :].astype(f32) - dot(tb[0, r, :], zb[1])
        full[r, :] = h
        tb[1, r, :] = h.astype(bf16)
    for r in halves:
        up_ref[0, r, :] = (8.0 * full[r, :] - dot(zb[0, r, :], tb[1])) * scale

    @pl.when(s > 0)
    def _():
        def left(step, carry):
            chain_copy(step // per, lax.rem(step, per)).wait_send()
            return carry

        lax.fori_loop(0, micro * per, left, 0)

    def drain(t, carry):
        for k in each:
            ring_copy(0, t, k).wait_send()
            pass_on(0, t, k).wait_send()
        return carry

    lax.fori_loop(0, half, drain, 0)

    def drain_down(t, carry):
        for k in each:
            ring_copy(1, t + 1, k).wait_send()
            pass_on(1, t, k).wait_send()
        return carry

    lax.fori_loop(0, half - 1, drain_down, 0)

    def drain_direct(d, carry):
        a_copy(d).wait_send()
        b_copy(d).wait_send()
        return carry

    lax.fori_loop(1, size, drain_direct, 0)
    ax_copy.wait_send()
    for k in each:
        over_copy(k).wait_send()


def body(rings, acts, weights, cot_last):
    sections = lax.axis_size("section")
    size = lax.axis_size("dp") // rings
    _, micro, rows, width = acts.shape
    nb = width // T
    tri = nb * (nb + 1) // 2 * T
    total = tri + nb * nb * T
    piece = total // size
    half = size // 2
    parts = len(pieces_of(width, size))
    vmem = pl.BlockSpec(memory_space=pltpu.VMEM)
    anywhere = pl.BlockSpec(memory_space=pl.ANY)
    bf16, f32 = jnp.bfloat16, jnp.float32
    dma = pltpu.SemaphoreType.DMA
    return pl.pallas_call(
        functools.partial(kernel, sections, rings, size),
        name="relay",
        out_shape=(
            jax.ShapeDtypeStruct((1, micro, rows, width), bf16),
            jax.ShapeDtypeStruct((1, width, width), f32),
        ),
        in_specs=[anywhere] * 3,
        out_specs=(vmem, vmem),
        scratch_shapes=[
            pltpu.VMEM((micro, rows, width), bf16),
            pltpu.VMEM((width, width), bf16),
            pltpu.VMEM((micro, rows, width), f32),
            pltpu.VMEM((width, micro * rows), bf16),
            pltpu.VMEM((micro, rows, width), bf16),
            pltpu.VMEM((micro * rows, width), bf16),
            pltpu.VMEM((total, T), f32),
            pltpu.VMEM((2, half, piece, T), bf16),
            pltpu.VMEM((2, half, piece, T), bf16),
            pltpu.VMEM((total, T), bf16),
            pltpu.VMEM((piece, T), bf16),
            pltpu.VMEM((piece, T), bf16),
            pltpu.VMEM((tri, T), bf16),
            pltpu.VMEM((size, tri // size, T), bf16),
            pltpu.VMEM((tri, T), bf16),
            pltpu.VMEM((tri // size, T), bf16),
            pltpu.VMEM((tri // size, T), bf16),
            pltpu.VMEM((width, width), f32),
            pltpu.VMEM((3, width, width), bf16),
            pltpu.VMEM((2, width, width), f32),
            pltpu.VMEM((2, width, width), bf16),
            dma((3,)),
            dma((micro, rows // ROWS)), dma((micro, rows // ROWS)),
            dma((2, half, parts)), dma((2, half, parts)),
            dma((2, parts)),
            dma((2, half, parts)), dma((2, half, parts)),
            dma((size,)), dma((size,)), dma((size,)), dma((size,)),
            dma((2,)),
        ],
        compiler_params=pltpu.CompilerParams(
            collective_id=0, has_side_effects=True, vmem_limit_bytes=40 << 20
        ),
    )(acts, weights, cot_last)


def solution(mesh):
    placed = (P("section", None, "dp", None), P("section", None, None), P(None, "dp", None))
    return jax.shard_map(
        functools.partial(body, 2),
        mesh=mesh,
        in_specs=placed,
        out_specs=(P("section", None, "dp", None), P("section", None, None)),
        check_vma=False,
    )
```

```python
import functools

import jax
import jax.numpy as jnp
from jax import lax
from jax.experimental import pallas as pl
from jax.experimental.pallas import tpu as pltpu
from jax.sharding import PartitionSpec as P

MESH = pl.DeviceIdType.MESH
T = 128
ROWS = 16
STAGES = 4


def dot(a, b):
    return jnp.dot(a, b, preferred_element_type=jnp.float32)


def ring_of(width, size):
    nb = width // T
    tri, square = nb * (nb + 1) // 2 * T, nb * nb * T
    o, g = tri // size, square // size
    return ((o, 0, 0),), ((o, 0, 0), (g, o, tri))


def kernel(
    sections, rings, size,
    acts_hbm, w_hbm, cot_hbm, dx_hbm, up_ref,
    x_ref, w2, x2, slope, xt, dyin, dhl, dxl, rdh, rdx,
    a_own, a_cst, a_crb, a_orb, a_red, a_xs, a_xr,
    b_own, b_cst, b_crb, b_orb, b_red, b_xs, b_xr,
    full, tb, ub, zb, inv,
    in_sem, pair_sem, dh_send, dh_recv, c_send, c_recv,
    a_sem, a_xsem, b_sem, b_xsem,
):
    s = lax.axis_index("section")
    p = lax.axis_index("dp")
    z, ring = lax.rem(p, size), p // size
    base = ring * size
    core, chip = lax.rem(s, 2), s // 2
    chips = sections // 2
    width = w2.shape[1]
    nb = width // T
    tri = nb * (nb + 1) // 2 * T
    rows = dyin.shape[0]
    micro = x_ref.shape[0]
    count = micro * rows * rings * size
    f32, bf16 = jnp.float32, jnp.bfloat16

    def along(d):
        return (s, base + lax.rem(z + size + d, size))

    over = (s, lax.rem(p + size, rings * size))
    partner = (s + 1 - 2 * core, p)

    barrier = pltpu.get_barrier_semaphore()
    peers = (along(1), along(-1), along(2), along(-2), over, partner, (lax.rem(s + 2, sections), p))
    for peer in peers:
        pl.semaphore_signal(barrier, inc=1, device_id=peer, device_id_type=MESH)

    get_x = pltpu.make_async_copy(acts_hbm.at[0], x_ref, in_sem.at[0])
    get_w = pltpu.make_async_copy(w_hbm.at[0], w2.at[core], in_sem.at[1])
    get_c = pltpu.make_async_copy(cot_hbm.at[core], dyin, in_sem.at[2])
    get_x.start()
    get_w.start()

    @pl.when(chip == chips - 1)
    def _():
        get_c.start()

    get_x.wait()
    get_w.wait()
    pl.semaphore_wait(barrier, len(peers))

    def pair_copy(src, dst, i):
        return pltpu.make_async_remote_copy(
            src_ref=src, dst_ref=dst, send_sem=pair_sem.at[0, i], recv_sem=pair_sem.at[1, i],
            device_id=partner, device_id_type=MESH,
        )

    x_copy = pair_copy(x_ref.at[1 - core], x2, 0)
    w_copy = pair_copy(w2.at[core], w2.at[core], 1)
    w_here = pair_copy(w2.at[1 - core], w2.at[1 - core], 1)
    x_copy.start()
    w_copy.start()

    def slope_of(x, which):
        pre = dot(x, w2[which])
        sig = 1.0 / (1.0 + jnp.exp(-pre))
        slope[which] = sig * (1.0 + pre * (1.0 - sig))

    slope_of(x_ref[core], core)
    x_copy.wait_recv()
    w_here.wait_recv()
    slope_of(x2[...], 1 - core)

    def upper(left, right, dst):
        at = 0
        for i in range(nb):
            prod = dot(left[i * T:(i + 1) * T, :], right[:, i * T:]).astype(bf16)
            for j in range(nb - i):
                dst[(at + j) * T:(at + j + 1) * T, :] = prod[:, j * T:(j + 1) * T]
            at += nb - i

    def act_sum():
        x = jnp.concatenate([x_ref[core], x_ref[1 - core]], axis=0)
        xt[...] = x.T
        upper(xt, x, a_own)

    def make_ring(pieces, own, cst, crb, orb, red, xs, xr, sem, xsem):
        each = range(len(pieces))

        def rows_of(chunk, k):
            n, _, first = pieces[k]
            return pl.ds(pl.multiple_of(first + lax.rem(chunk + size, size) * n, 16), n)

        def part(k):
            n, first, _ = pieces[k]
            return slice(first, first + n)

        def slot(k):
            n, first, _ = pieces[k]
            return pl.ds(first, n)

        def copy(kind, src, dst, way, t, k):
            step = (2, 1, 2, 1)[kind]
            return pltpu.make_async_remote_copy(
                src_ref=src, dst_ref=dst,
                send_sem=sem.at[0, kind, way, t, k], recv_sem=sem.at[1, kind, way, t, k],
                device_id=along(step if way == 0 else -step), device_id_type=MESH,
            )

        def sign(way, d):
            return z + d if way == 0 else z - d

        def chain(way, t, k):
            return copy(0, cst.at[way, t, slot(k), :], crb.at[way, t, slot(k), :], way, t, k)

        def odd(way, t, k):
            mine = own.at[rows_of(sign(way, 2 * STAGES - 1 - 2 * t), k), :]
            return copy(1, mine, orb.at[way, t, slot(k), :], way, t, k)

        def spread(kind, way, t, k, chunk):
            there = red.at[rows_of(chunk, k), :]
            return copy(kind, there, there, way, t, k)

        def sent(kind, way, t, k):
            return spread(kind, way, t, k, sign(way, -2 * t))

        def arrived(kind, way, t, k):
            return spread(kind, way, t, k, sign(way, -2 * t - (2, 1)[kind - 2]))

        def across(k):
            return pltpu.make_async_remote_copy(
                src_ref=xs.at[slot(k), :], dst_ref=xr.at[slot(k), :],
                send_sem=xsem.at[0, k], recv_sem=xsem.at[1, k],
                device_id=over, device_id_type=MESH,
            )

        def collect(value, way, t, k, chained):
            odd(way, t, k).wait_recv()
            value = value + orb[way, t, part(k), :].astype(f32)
            if chained:
                chain(way, t, k).wait_recv()
                value = value + crb[way, t, part(k), :].astype(f32)
            return value

        def first():
            for k in each:
                cst[0, 0, part(k), :] = own[rows_of(z + 2 * STAGES, k), :]
                chain(0, 0, k).start()
                for way in range(2):
                    odd(way, 0, k).start()

        def middle(t, chained):
            for k in each:
                for way in range(2):
                    odd(way, t, k).start()
            for k in each:
                for way in range(2):
                    value = own[rows_of(sign(way, 2 * STAGES - 2 * t), k), :].astype(f32)
                    value = collect(value, way, t - 1, k, chained[way])
                    cst[way, t, part(k), :] = value.astype(bf16)
                    chain(way, t, k).start()

        def owner():
            for k in each:
                value = own[rows_of(z, k), :].astype(f32)
                for way in range(2):
                    value = collect(value, way, STAGES - 1, k, True)
                xs[part(k), :] = value.astype(bf16)
                across(k).start()

        def start_gather():
            for k in each:
                across(k).wait_recv()
                total = xs[part(k), :].astype(f32) + xr[part(k), :].astype(f32)
                red[rows_of(z, k), :] = total.astype(bf16)
                for kind in (2, 3):
                    for way in range(2):
                        sent(kind, way, 0, k).start()

        def pass_on(t, ways):
            for k in each:
                for way in range(2):
                    arrived(2, way, t - 1, k).wait_recv()
                    if way in ways:
                        sent(2, way, t, k).start()
                    sent(3, way, t, k).start()

        def stage(t):
            pl.when(t == 0)(first)
            pl.when(t == 1)(lambda: middle(1, (True, False)))
            pl.when(jnp.logical_and(t > 1, t < STAGES))(lambda: middle(t, (True, True)))
            pl.when(t == STAGES)(owner)
            pl.when(t == STAGES + 1)(start_gather)
            pl.when(jnp.logical_and(t > STAGES + 1, t < 2 * STAGES))(
                lambda: pass_on(t - STAGES - 1, (0, 1))
            )
            pl.when(t == 2 * STAGES)(lambda: pass_on(STAGES - 1, (0,)))

        def finish(k):
            for t in range(STAGES):
                for way in range(2):
                    arrived(3, way, t, k).wait_recv()
            arrived(2, 0, STAGES - 1, k).wait_recv()

        def drain():
            for k in each:
                for way in range(2):
                    def left(t, carry):
                        odd(way, t, k).wait_send()
                        sent(3, way, t, k).wait_send()
                        return carry

                    def left_two(t, carry):
                        chain(way, t + way, k).wait_send()
                        sent(2, way, t, k).wait_send()
                        return carry

                    lax.fori_loop(0, STAGES, left, 0)
                    lax.fori_loop(0, STAGES - way, left_two, 0)
                across(k).wait_send()

        return stage, finish, drain

    a_pieces, b_pieces = ring_of(width, size)
    a_stage, a_finish, a_drain = make_ring(
        a_pieces, a_own, a_cst, a_crb, a_orb, a_red, a_xs, a_xr, a_sem, a_xsem
    )
    b_stage, b_finish, b_drain = make_ring(
        b_pieces, b_own, b_cst, b_crb, b_orb, b_red, b_xs, b_xr, b_sem, b_xsem
    )

    ahead = chips - 1 - chip

    def a_ahead(t, carry):
        a_stage(t)
        return carry

    @pl.when(chip < chips - 1)
    def _():
        act_sum()

    lax.fori_loop(0, ahead, a_ahead, 0)

    def chain_copy(r):
        at = pl.ds(pl.multiple_of(r * ROWS, ROWS), ROWS)
        return pltpu.make_async_remote_copy(
            src_ref=dxl.at[0, at, :], dst_ref=dyin.at[at, :],
            send_sem=c_send.at[r], recv_sem=c_recv.at[r],
            device_id=(s - 2, p), device_id_type=MESH,
        )

    def dh_copy(r):
        at = pl.ds(pl.multiple_of(r * ROWS, ROWS), ROWS)
        return pltpu.make_async_remote_copy(
            src_ref=dhl.at[1 - core, at, :], dst_ref=rdh.at[at, :],
            send_sem=dh_send.at[r], recv_sem=dh_recv.at[r],
            device_id=partner, device_id_type=MESH,
        )

    @pl.when(chip == chips - 1)
    def _():
        get_c.wait()

    def relay(r, carry):
        @pl.when(chip < chips - 1)
        def _():
            chain_copy(r).wait_recv()

        at = pl.ds(pl.multiple_of(r * ROWS, ROWS), ROWS)
        dy = dyin[at, :].astype(f32)
        for which in (1, 0):
            part = (dy * slope[which, at, :]).astype(bf16)
            dhl[which, at, :] = part
            back = lax.dot_general(
                part, w2[which], (((1,), (1,)), ((), ())), preferred_element_type=f32
            )
            result = (dy + back).astype(bf16)
            dxl[which, at, :] = result
            dy = result.astype(f32)

        @pl.when(chip > 0)
        def _():
            chain_copy(r).start()

        dh_copy(r).start()
        return carry

    lax.fori_loop(0, rows // ROWS, relay, 0)
    dx_copy = pair_copy(dxl.at[1 - core], rdx, 2)
    dx_copy.start()

    @pl.when(chip == chips - 1)
    def _():
        act_sum()

    def dh_wait(r, carry):
        dh_copy(r).wait_recv()
        return carry

    lax.fori_loop(0, rows // ROWS, dh_wait, 0)
    d = jnp.concatenate([dhl[core], rdh[...]], axis=0)
    upper(d.T, d, b_own)
    for i in range(nb):
        prod = dot(xt[i * T:(i + 1) * T, :], d).astype(bf16)
        for j in range(nb):
            b_own[tri + (i * nb + j) * T:tri + (i * nb + j + 1) * T, :] = prod[:, j * T:(j + 1) * T]

    put_mine = pltpu.make_async_copy(dxl.at[core], dx_hbm.at[0, core], in_sem.at[3])
    put_theirs = pltpu.make_async_copy(rdx, dx_hbm.at[0, 1 - core], in_sem.at[4])

    halves = [slice(h * (width // 2), (h + 1) * (width // 2)) for h in range(2)]

    def newton(src, side):
        at = 0
        for i in range(nb):
            for j in range(i, nb):
                block = src[at * T:(at + 1) * T, :].astype(f32) / count
                if i == j:
                    row = lax.broadcasted_iota(jnp.int32, (T, T), 0)
                    col = lax.broadcasted_iota(jnp.int32, (T, T), 1)
                    block = block + jnp.where(row == col, 0.01, 0.0)
                else:
                    full[j * T:(j + 1) * T, i * T:(i + 1) * T] = block.T
                full[i * T:(i + 1) * T, j * T:(j + 1) * T] = block
                at += 1
        m = full[...]
        scale = 1.0 / jnp.sqrt(jnp.sum(m * m, keepdims=True))
        inv[side] = jnp.broadcast_to(scale, inv.shape[1:])
        t = m * scale
        full[...] = t
        tb[0] = t.astype(bf16)
        for r in halves:
            u = 2.0 * full[r, :] - dot(tb[0, r, :], tb[0])
            ub[0, r, :] = u
            tb[1, r, :] = u.astype(bf16)
        for r in halves:
            v = 2.0 * ub[0, r, :] - dot(tb[1, r, :], tb[1])
            ub[1, r, :] = v
            tb[2, r, :] = v.astype(bf16)
        for r in halves:
            y = 2.0 * (full[r, :] + ub[0, r, :]) - dot(tb[0, r, :], tb[1])
            last = 4.0 * ub[1, r, :] + 2.0 * y - dot(y.astype(bf16), tb[2])
            zb[side, r, :] = last.astype(bf16)

    last = 2 * STAGES
    early = ahead >= STAGES

    def both(t, carry):
        b_stage(t)

        @pl.when(ahead + t <= last)
        def _():
            a_stage(ahead + t)

        @pl.when(jnp.logical_and(early, t == last - 2))
        def _():
            for k in range(len(a_pieces)):
                a_finish(k)
            newton(a_red, 0)

        return carry

    lax.fori_loop(0, last + 1, both, 0)

    @pl.when(jnp.logical_not(early))
    def _():
        for k in range(len(a_pieces)):
            a_finish(k)
        newton(a_red, 0)

    dx_copy.wait_recv()
    put_mine.start()
    put_theirs.start()
    b_finish(0)
    newton(b_red, 1)
    b_finish(1)
    for i in range(nb):
        for j in range(nb):
            block = b_red[tri + (i * nb + j) * T:tri + (i * nb + j + 1) * T, :]
            tb[0, i * T:(i + 1) * T, j * T:(j + 1) * T] = block
    scale = inv[0, 0:1, 0:1] * inv[1, 0:1, 0:1]
    for r in halves:
        h = 8.0 * tb[0, r, :].astype(f32) - dot(tb[0, r, :], zb[1])
        full[r, :] = h
        tb[1, r, :] = h.astype(bf16)
    for r in halves:
        up_ref[0, r, :] = (8.0 * full[r, :] - dot(zb[0, r, :], tb[1])) * scale

    def left(r, carry):
        dh_copy(r).wait_send()
        return carry

    lax.fori_loop(0, rows // ROWS, left, 0)

    @pl.when(chip > 0)
    def _():
        def left(r, carry):
            chain_copy(r).wait_send()
            return carry

        lax.fori_loop(0, rows // ROWS, left, 0)

    a_drain()
    b_drain()
    x_copy.wait_send()
    w_copy.wait_send()
    dx_copy.wait_send()
    put_mine.wait()
    put_theirs.wait()


def body(rings, acts, weights, cot_last):
    sections = lax.axis_size("section")
    size = lax.axis_size("dp") // rings
    _, micro, rows, width = acts.shape
    vmem = pl.BlockSpec(memory_space=pltpu.VMEM)
    hbm = pl.BlockSpec(memory_space=pltpu.HBM)
    bf16, f32 = jnp.bfloat16, jnp.float32
    dma = pltpu.SemaphoreType.DMA

    def ring_scratch(pieces):
        piece = sum(n for n, _, _ in pieces)
        passing = pltpu.VMEM((2, STAGES, piece, T), bf16)
        whole = pltpu.VMEM((piece * size, T), bf16)
        message = pltpu.VMEM((piece, T), bf16)
        return [whole, passing, passing, passing, whole, message, message]

    a_pieces, b_pieces = ring_of(width, size)
    return pl.pallas_call(
        functools.partial(kernel, sections, rings, size),
        name="relay",
        out_shape=(
            jax.ShapeDtypeStruct((1, micro, rows, width), bf16),
            jax.ShapeDtypeStruct((1, width, width), f32),
        ),
        in_specs=[hbm] * 3,
        out_specs=(hbm, vmem),
        scratch_shapes=[
            pltpu.VMEM((micro, rows, width), bf16),
            pltpu.VMEM((2, width, width), bf16),
            pltpu.VMEM((rows, width), bf16),
            pltpu.VMEM((2, rows, width), f32),
            pltpu.VMEM((width, micro * rows), bf16),
            pltpu.VMEM((rows, width), bf16),
            pltpu.VMEM((2, rows, width), bf16),
            pltpu.VMEM((2, rows, width), bf16),
            pltpu.VMEM((rows, width), bf16),
            pltpu.VMEM((rows, width), bf16),
            *ring_scratch(a_pieces),
            *ring_scratch(b_pieces),
            pltpu.VMEM((width, width), f32),
            pltpu.VMEM((3, width, width), bf16),
            pltpu.VMEM((2, width, width), f32),
            pltpu.VMEM((2, width, width), bf16),
            pltpu.VMEM((2, 8, T), f32),
            dma((5,)), dma((2, 3)),
            dma((rows // ROWS,)), dma((rows // ROWS,)),
            dma((rows // ROWS,)), dma((rows // ROWS,)),
            dma((2, 4, 2, STAGES, len(a_pieces))), dma((2, len(a_pieces))),
            dma((2, 4, 2, STAGES, len(b_pieces))), dma((2, len(b_pieces))),
        ],
        compiler_params=pltpu.CompilerParams(
            collective_id=0, has_side_effects=True, vmem_limit_bytes=63 << 20
        ),
    )(acts, weights, cot_last)


def solution(mesh):
    placed = (P("section", None, "dp", None), P("section", None, None), P(None, "dp", None))
    return jax.shard_map(
        functools.partial(body, 2),
        mesh=mesh,
        in_specs=placed,
        out_specs=(P("section", None, "dp", None), P("section", None, None)),
        check_vma=False,
    )
```

```python
import functools

import jax
import jax.numpy as jnp
from jax import lax
from jax.experimental import pallas as pl
from jax.experimental.pallas import tpu as pltpu
from jax.sharding import PartitionSpec as P

MESH = pl.DeviceIdType.MESH
T = 128
ROWS = 16
STAGES = 4


def dot(a, b):
    return jnp.dot(a, b, preferred_element_type=jnp.float32)


def ring_of(width, size):
    nb = width // T
    tri, square = nb * (nb + 1) // 2 * T, nb * nb * T
    o, g = tri // size, square // size
    return ((o, 0, 0),), ((o, 0, 0), (g, o, tri))


def kernel(
    sections, rings, size,
    acts_hbm, w_hbm, cot_hbm, dx_ref, h_ref, za_ref,
    x_ref, w2, wt, x2, slope, xt, dyin, dhl, dxl, rdh, rdx,
    a_own, a_cst, a_crb, a_orb, a_red, a_xs, a_xr,
    b_own, b_cst, b_crb, b_orb, b_red, b_xs, b_xr,
    full, tb, ub, zb, inv,
    in_sem, pair_sem, dh_send, dh_recv, c_send, c_recv,
    a_sem, a_xsem, b_sem, b_xsem,
):
    s = lax.axis_index("section")
    p = lax.axis_index("dp")
    z, ring = lax.rem(p, size), p // size
    base = ring * size
    core, chip = lax.rem(s, 2), s // 2
    chips = sections // 2
    mine = lax.rem(core + chips - 1 - chip, 2)
    width = w2.shape[1]
    nb = width // T
    tri = nb * (nb + 1) // 2 * T
    rows = dyin.shape[0]
    micro = x_ref.shape[0]
    count = micro * rows * rings * size
    f32, bf16 = jnp.float32, jnp.bfloat16

    def along(d):
        return (s, base + lax.rem(z + size + d, size))

    over = (s, lax.rem(p + size, rings * size))
    partner = (s + 1 - 2 * core, p)

    barrier = pltpu.get_barrier_semaphore()
    peers = (along(1), along(-1), along(2), along(-2), over, partner, (2 * lax.rem(chip + 1, chips) + 1 - core, p))
    for peer in peers:
        pl.semaphore_signal(barrier, inc=1, device_id=peer, device_id_type=MESH)

    get_x = pltpu.make_async_copy(acts_hbm.at[0], x_ref, in_sem.at[0])
    get_w = pltpu.make_async_copy(w_hbm.at[0], w2.at[core], in_sem.at[1])
    get_c = pltpu.make_async_copy(cot_hbm.at[mine], dyin, in_sem.at[2])
    get_x.start()
    get_w.start()

    @pl.when(chip == chips - 1)
    def _():
        get_c.start()

    get_x.wait()
    get_w.wait()
    pl.semaphore_wait(barrier, len(peers))

    def pair_copy(src, dst, i):
        return pltpu.make_async_remote_copy(
            src_ref=src, dst_ref=dst, send_sem=pair_sem.at[0, i], recv_sem=pair_sem.at[1, i],
            device_id=partner, device_id_type=MESH,
        )

    x_copy = pair_copy(x_ref.at[1 - mine], x2, 0)
    w_copy = pair_copy(w2.at[core], w2.at[core], 1)
    w_here = pair_copy(w2.at[1 - core], w2.at[1 - core], 1)
    x_copy.start()
    w_copy.start()

    def slope_of(x, which):
        pre = dot(x, w2[which])
        sig = 1.0 / (1.0 + jnp.exp(-pre))
        slope[which] = sig * (1.0 + pre * (1.0 - sig))

    slope_of(x_ref[mine], core)
    wt[core] = w2[core].T
    x_copy.wait_recv()
    w_here.wait_recv()
    slope_of(x2[...], 1 - core)
    wt[1 - core] = w2[1 - core].T

    def upper(left, right, dst):
        at = 0
        for i in range(nb):
            prod = dot(left[i * T:(i + 1) * T, :], right[:, i * T:]).astype(bf16)
            for j in range(nb - i):
                dst[(at + j) * T:(at + j + 1) * T, :] = prod[:, j * T:(j + 1) * T]
            at += nb - i

    def act_sum():
        x = jnp.concatenate([x_ref[mine], x_ref[1 - mine]], axis=0)
        xt[...] = x.T
        upper(xt, x, a_own)

    def make_ring(pieces, own, cst, crb, orb, red, xs, xr, sem, xsem):
        each = range(len(pieces))

        def rows_of(chunk, k):
            n, _, first = pieces[k]
            return pl.ds(pl.multiple_of(first + lax.rem(chunk + size, size) * n, 16), n)

        def part(k):
            n, first, _ = pieces[k]
            return slice(first, first + n)

        def slot(k):
            n, first, _ = pieces[k]
            return pl.ds(first, n)

        def copy(kind, src, dst, way, t, k):
            step = (2, 1, 2, 1)[kind]
            return pltpu.make_async_remote_copy(
                src_ref=src, dst_ref=dst,
                send_sem=sem.at[0, kind, way, t, k], recv_sem=sem.at[1, kind, way, t, k],
                device_id=along(step if way == 0 else -step), device_id_type=MESH,
            )

        def sign(way, d):
            return z + d if way == 0 else z - d

        def chain(way, t, k):
            return copy(0, cst.at[way, t, slot(k), :], crb.at[way, t, slot(k), :], way, t, k)

        def odd(way, t, k):
            mine = own.at[rows_of(sign(way, 2 * STAGES - 1 - 2 * t), k), :]
            return copy(1, mine, orb.at[way, t, slot(k), :], way, t, k)

        def spread(kind, way, t, k, chunk):
            there = red.at[rows_of(chunk, k), :]
            return copy(kind, there, there, way, t, k)

        def sent(kind, way, t, k):
            return spread(kind, way, t, k, sign(way, -2 * t))

        def arrived(kind, way, t, k):
            return spread(kind, way, t, k, sign(way, -2 * t - (2, 1)[kind - 2]))

        def across(k):
            return pltpu.make_async_remote_copy(
                src_ref=xs.at[slot(k), :], dst_ref=xr.at[slot(k), :],
                send_sem=xsem.at[0, k], recv_sem=xsem.at[1, k],
                device_id=over, device_id_type=MESH,
            )

        def collect(value, way, t, k, chained):
            odd(way, t, k).wait_recv()
            value = value + orb[way, t, part(k), :].astype(f32)
            if chained:
                chain(way, t, k).wait_recv()
                value = value + crb[way, t, part(k), :].astype(f32)
            return value

        def first(k):
            cst[0, 0, part(k), :] = own[rows_of(z + 2 * STAGES, k), :]
            chain(0, 0, k).start()
            for way in range(2):
                odd(way, 0, k).start()

        def all_first():
            for k in each:
                first(k)

        def middle(t, chained):
            for k in each:
                for way in range(2):
                    odd(way, t, k).start()
            for k in each:
                for way in range(2):
                    value = own[rows_of(sign(way, 2 * STAGES - 2 * t), k), :].astype(f32)
                    value = collect(value, way, t - 1, k, chained[way])
                    cst[way, t, part(k), :] = value.astype(bf16)
                    chain(way, t, k).start()

        def owner():
            for k in each:
                value = own[rows_of(z, k), :].astype(f32)
                for way in range(2):
                    value = collect(value, way, STAGES - 1, k, True)
                xs[part(k), :] = value.astype(bf16)
                across(k).start()

        def start_gather():
            for k in each:
                across(k).wait_recv()
                total = xs[part(k), :].astype(f32) + xr[part(k), :].astype(f32)
                red[rows_of(z, k), :] = total.astype(bf16)
                for kind in (2, 3):
                    for way in range(2):
                        sent(kind, way, 0, k).start()

        def pass_on(t, ways):
            for k in each:
                for way in range(2):
                    arrived(2, way, t - 1, k).wait_recv()
                    if way in ways:
                        sent(2, way, t, k).start()
                    sent(3, way, t, k).start()

        def stage(t, begun=False):
            if not begun:
                pl.when(t == 0)(all_first)
            pl.when(t == 1)(lambda: middle(1, (True, False)))
            pl.when(jnp.logical_and(t > 1, t < STAGES))(lambda: middle(t, (True, True)))
            pl.when(t == STAGES)(owner)
            pl.when(t == STAGES + 1)(start_gather)
            pl.when(jnp.logical_and(t > STAGES + 1, t < 2 * STAGES))(
                lambda: pass_on(t - STAGES - 1, (0, 1))
            )
            pl.when(t == 2 * STAGES)(lambda: pass_on(STAGES - 1, (0,)))

        def finish(k):
            for t in range(STAGES):
                for way in range(2):
                    arrived(3, way, t, k).wait_recv()
            arrived(2, 0, STAGES - 1, k).wait_recv()

        def drain():
            for k in each:
                for way in range(2):
                    def left(t, carry):
                        odd(way, t, k).wait_send()
                        sent(3, way, t, k).wait_send()
                        return carry

                    def left_two(t, carry):
                        chain(way, t + way, k).wait_send()
                        sent(2, way, t, k).wait_send()
                        return carry

                    lax.fori_loop(0, STAGES, left, 0)
                    lax.fori_loop(0, STAGES - way, left_two, 0)
                across(k).wait_send()

        return first, stage, finish, drain

    a_pieces, b_pieces = ring_of(width, size)
    _, a_stage, a_finish, a_drain = make_ring(
        a_pieces, a_own, a_cst, a_crb, a_orb, a_red, a_xs, a_xr, a_sem, a_xsem
    )
    b_first, b_stage, b_finish, b_drain = make_ring(
        b_pieces, b_own, b_cst, b_crb, b_orb, b_red, b_xs, b_xr, b_sem, b_xsem
    )

    ahead = chips - 1 - chip

    def a_ahead(t, carry):
        a_stage(t)
        return carry

    @pl.when(chip < chips - 1)
    def _():
        act_sum()

    lax.fori_loop(0, ahead, a_ahead, 0)

    def chain_copy(r):
        at = pl.ds(pl.multiple_of(r * ROWS, ROWS), ROWS)
        return pltpu.make_async_remote_copy(
            src_ref=dxl.at[0, at, :], dst_ref=dyin.at[at, :],
            send_sem=c_send.at[r], recv_sem=c_recv.at[r],
            device_id=(2 * chip - 1 - core, p), device_id_type=MESH,
        )

    def dh_copy(r):
        at = pl.ds(pl.multiple_of(r * ROWS, ROWS), ROWS)
        return pltpu.make_async_remote_copy(
            src_ref=dhl.at[1 - core, at, :], dst_ref=rdh.at[at, :],
            send_sem=dh_send.at[r], recv_sem=dh_recv.at[r],
            device_id=partner, device_id_type=MESH,
        )

    @pl.when(chip == chips - 1)
    def _():
        get_c.wait()

    def relay(r, carry):
        @pl.when(chip < chips - 1)
        def _():
            chain_copy(r).wait_recv()

        at = pl.ds(pl.multiple_of(r * ROWS, ROWS), ROWS)
        dy = dyin[at, :].astype(f32)
        for which in (1, 0):
            part = (dy * slope[which, at, :]).astype(bf16)
            dhl[which, at, :] = part
            result = (dy + dot(part, wt[which])).astype(bf16)
            dxl[which, at, :] = result
            dy = result.astype(f32)

        @pl.when(chip > 0)
        def _():
            chain_copy(r).start()

        dh_copy(r).start()
        return carry

    lax.fori_loop(0, rows // ROWS, relay, 0)
    dx_copy = pair_copy(dxl.at[1 - core], rdx, 2)
    dx_copy.start()

    @pl.when(chip == chips - 1)
    def _():
        act_sum()

    def dh_wait(r, carry):
        dh_copy(r).wait_recv()
        return carry

    lax.fori_loop(0, rows // ROWS, dh_wait, 0)
    d = jnp.concatenate([dhl[core], rdh[...]], axis=0)
    upper(d.T, d, b_own)
    b_first(0)
    for i in range(nb):
        prod = dot(xt[i * T:(i + 1) * T, :], d).astype(bf16)
        for j in range(nb):
            b_own[tri + (i * nb + j) * T:tri + (i * nb + j + 1) * T, :] = prod[:, j * T:(j + 1) * T]
    b_first(1)

    put_mine = pltpu.make_async_copy(dxl.at[core], dx_ref.at[0, mine], in_sem.at[3])
    put_theirs = pltpu.make_async_copy(rdx, dx_ref.at[0, 1 - mine], in_sem.at[4])

    halves = [slice(h * (width // 2), (h + 1) * (width // 2)) for h in range(2)]

    def newton(src, side, dst):
        at = 0
        for i in range(nb):
            for j in range(i, nb):
                block = src[at * T:(at + 1) * T, :].astype(f32) / count
                if i == j:
                    row = lax.broadcasted_iota(jnp.int32, (T, T), 0)
                    col = lax.broadcasted_iota(jnp.int32, (T, T), 1)
                    block = block + jnp.where(row == col, 0.01, 0.0)
                else:
                    full[j * T:(j + 1) * T, i * T:(i + 1) * T] = block.T
                full[i * T:(i + 1) * T, j * T:(j + 1) * T] = block
                at += 1
        m = full[...]
        scale = 1.0 / jnp.sqrt(jnp.sum(m * m, keepdims=True))
        inv[side] = jnp.broadcast_to(scale, inv.shape[1:])
        t = m * scale
        full[...] = t
        tb[0] = t.astype(bf16)
        for r in halves:
            u = 2.0 * full[r, :] - dot(tb[0, r, :], tb[0])
            ub[0, r, :] = u
            tb[1, r, :] = u.astype(bf16)
        for r in halves:
            v = 2.0 * ub[0, r, :] - dot(tb[1, r, :], tb[1])
            ub[1, r, :] = v
            tb[2, r, :] = v.astype(bf16)
        for r in halves:
            y = 2.0 * (full[r, :] + ub[0, r, :]) - dot(tb[0, r, :], tb[1])
            last = 4.0 * ub[1, r, :] + 2.0 * y - dot(y.astype(bf16), tb[2])
            dst[r, :] = last.astype(bf16)

    last = 2 * STAGES
    early = ahead > STAGES

    def both(t, carry):
        b_stage(t, True)

        @pl.when(ahead + t <= last)
        def _():
            a_stage(ahead + t)

        @pl.when(jnp.logical_and(early, t == STAGES))
        def _():
            for k in range(len(a_pieces)):
                a_finish(k)
            newton(a_red, 0, za_ref)

        return carry

    lax.fori_loop(0, last + 1, both, 0)

    @pl.when(jnp.logical_not(early))
    def _():
        for k in range(len(a_pieces)):
            a_finish(k)
        newton(a_red, 0, za_ref)

    dx_copy.wait_recv()
    put_mine.start()
    put_theirs.start()
    b_finish(0)
    newton(b_red, 1, zb)
    b_finish(1)
    for i in range(nb):
        for j in range(nb):
            block = b_red[tri + (i * nb + j) * T:tri + (i * nb + j + 1) * T, :]
            tb[0, i * T:(i + 1) * T, j * T:(j + 1) * T] = block
    scale = inv[0, 0:1, 0:1] * inv[1, 0:1, 0:1]
    for r in halves:
        h_ref[r, :] = (8.0 * tb[0, r, :].astype(f32) - dot(tb[0, r, :], zb[...])) * scale

    def left(r, carry):
        dh_copy(r).wait_send()
        return carry

    lax.fori_loop(0, rows // ROWS, left, 0)

    @pl.when(chip > 0)
    def _():
        def left(r, carry):
            chain_copy(r).wait_send()
            return carry

        lax.fori_loop(0, rows // ROWS, left, 0)

    a_drain()
    b_drain()
    x_copy.wait_send()
    w_copy.wait_send()
    dx_copy.wait_send()
    put_mine.wait()
    put_theirs.wait()


def finish_kernel(dx_ref, h_ref, za_ref, dx_hbm, up_hbm, up, sem):
    put_dx = pltpu.make_async_copy(dx_ref, dx_hbm, sem.at[0])
    put_dx.start()
    h = h_ref[...].astype(jnp.bfloat16)
    puts = []
    for i in range(up.shape[0] // T):
        r = slice(i * T, (i + 1) * T)
        up[r, :] = 8.0 * h_ref[r, :] - dot(za_ref[r, :], h)
        put = pltpu.make_async_copy(up.at[r, :], up_hbm.at[0, r, :], sem.at[1 + i])
        put.start()
        puts.append(put)
    put_dx.wait()
    for put in puts:
        put.wait()


def body(rings, acts, weights, cot_last):
    sections = lax.axis_size("section")
    size = lax.axis_size("dp") // rings
    _, micro, rows, width = acts.shape
    vmem = pl.BlockSpec(memory_space=pltpu.VMEM)
    hbm = pl.BlockSpec(memory_space=pltpu.HBM)
    bf16, f32 = jnp.bfloat16, jnp.float32
    dma = pltpu.SemaphoreType.DMA

    def ring_scratch(pieces):
        piece = sum(n for n, _, _ in pieces)
        passing = pltpu.VMEM((2, STAGES, piece, T), bf16)
        whole = pltpu.VMEM((piece * size, T), bf16)
        message = pltpu.VMEM((piece, T), bf16)
        return [whole, passing, passing, passing, whole, message, message]

    a_pieces, b_pieces = ring_of(width, size)
    dx, h, za = pl.pallas_call(
        functools.partial(kernel, sections, rings, size),
        name="relay",
        out_shape=(
            jax.ShapeDtypeStruct((1, micro, rows, width), bf16),
            jax.ShapeDtypeStruct((width, width), f32),
            jax.ShapeDtypeStruct((width, width), bf16),
        ),
        in_specs=[hbm] * 3,
        out_specs=(vmem, vmem, vmem),
        scratch_shapes=[
            pltpu.VMEM((micro, rows, width), bf16),
            pltpu.VMEM((2, width, width), bf16),
            pltpu.VMEM((2, width, width), bf16),
            pltpu.VMEM((rows, width), bf16),
            pltpu.VMEM((2, rows, width), f32),
            pltpu.VMEM((width, micro * rows), bf16),
            pltpu.VMEM((rows, width), bf16),
            pltpu.VMEM((2, rows, width), bf16),
            pltpu.VMEM((2, rows, width), bf16),
            pltpu.VMEM((rows, width), bf16),
            pltpu.VMEM((rows, width), bf16),
            *ring_scratch(a_pieces),
            *ring_scratch(b_pieces),
            pltpu.VMEM((width, width), f32),
            pltpu.VMEM((3, width, width), bf16),
            pltpu.VMEM((2, width, width), f32),
            pltpu.VMEM((width, width), bf16),
            pltpu.VMEM((2, 8, T), f32),
            dma((5,)), dma((2, 3)),
            dma((rows // ROWS,)), dma((rows // ROWS,)),
            dma((rows // ROWS,)), dma((rows // ROWS,)),
            dma((2, 4, 2, STAGES, len(a_pieces))), dma((2, len(a_pieces))),
            dma((2, 4, 2, STAGES, len(b_pieces))), dma((2, len(b_pieces))),
        ],
        compiler_params=pltpu.CompilerParams(
            collective_id=0, has_side_effects=True, vmem_limit_bytes=48 << 20
        ),
    )(*(pltpu.with_memory_space_constraint(a, pltpu.HBM) for a in (acts, weights, cot_last)))
    return pl.pallas_call(
        finish_kernel,
        name="finish",
        out_shape=(
            jax.ShapeDtypeStruct((1, micro, rows, width), bf16),
            jax.ShapeDtypeStruct((1, width, width), f32),
        ),
        in_specs=[vmem] * 3,
        out_specs=(hbm, hbm),
        scratch_shapes=[
            pltpu.VMEM((width, width), f32),
            dma((1 + width // T,)),
        ],
        compiler_params=pltpu.CompilerParams(vmem_limit_bytes=8 << 20),
    )(dx, h, za)


def solution(mesh):
    placed = (P("section", None, "dp", None), P("section", None, None), P(None, "dp", None))
    return jax.shard_map(
        functools.partial(body, 2),
        mesh=mesh,
        in_specs=placed,
        out_specs=(P("section", None, "dp", None), P("section", None, None)),
        check_vma=False,
    )
```

```python
import functools

import jax
import jax.numpy as jnp
from jax import lax
from jax.experimental import pallas as pl
from jax.experimental.pallas import tpu as pltpu
from jax.sharding import PartitionSpec as P

MESH = pl.DeviceIdType.MESH
T = 128
ROWS = 16
STAGES = 4


def dot(a, b):
    return jnp.dot(a, b, preferred_element_type=jnp.float32)


def ring_of(width, size):
    nb = width // T
    tri, square = nb * (nb + 1) // 2 * T, nb * nb * T
    o, g = tri // size, square // size
    return ((o, 0, 0),), ((o, 0, 0), (g, o, tri))


def kernel(
    sections, rings, size,
    acts_hbm, w_hbm, cot_hbm, dx_ref, h_ref, za_ref,
    x_ref, w2, wt, x2, slope, xt, dyin, dhl, dxl, rdh, rdx,
    a_own, a_cst, a_crb, a_orb, a_red, a_xs, a_xr,
    b_own, b_cst, b_crb, b_orb, b_red, b_xs, b_xr,
    full, tb, ub, zb, inv,
    in_sem, pair_sem, dh_send, dh_recv, c_send, c_recv,
    a_sem, a_xsem, b_sem, b_xsem,
):
    s = lax.axis_index("section")
    p = lax.axis_index("dp")
    z, ring = lax.rem(p, size), p // size
    base = ring * size
    core, chip = lax.rem(s, 2), s // 2
    chips = sections // 2
    mine = lax.rem(core + chips - 1 - chip, 2)
    width = w2.shape[1]
    nb = width // T
    tri = nb * (nb + 1) // 2 * T
    rows = dyin.shape[0]
    micro = x_ref.shape[0]
    count = micro * rows * rings * size
    f32, bf16 = jnp.float32, jnp.bfloat16

    def along(d):
        return (s, base + lax.rem(z + size + d, size))

    over = (s, lax.rem(p + size, rings * size))
    partner = (s + 1 - 2 * core, p)

    barrier = pltpu.get_barrier_semaphore()
    peers = (along(1), along(-1), along(2), along(-2), over, partner, (2 * lax.rem(chip + 1, chips) + 1 - core, p))
    for peer in peers:
        pl.semaphore_signal(barrier, inc=1, device_id=peer, device_id_type=MESH)

    get_x = pltpu.make_async_copy(acts_hbm.at[0], x_ref, in_sem.at[0])
    get_w = pltpu.make_async_copy(w_hbm.at[0], w2.at[core], in_sem.at[1])
    get_c = pltpu.make_async_copy(cot_hbm.at[mine], dyin, in_sem.at[2])
    get_x.start()
    get_w.start()

    @pl.when(chip == chips - 1)
    def _():
        get_c.start()

    get_x.wait()
    get_w.wait()
    pl.semaphore_wait(barrier, len(peers))

    def pair_copy(src, dst, i):
        return pltpu.make_async_remote_copy(
            src_ref=src, dst_ref=dst, send_sem=pair_sem.at[0, i], recv_sem=pair_sem.at[1, i],
            device_id=partner, device_id_type=MESH,
        )

    x_copy = pair_copy(x_ref.at[1 - mine], x2, 0)
    w_copy = pair_copy(w2.at[core], w2.at[core], 1)
    w_here = pair_copy(w2.at[1 - core], w2.at[1 - core], 1)
    x_copy.start()
    w_copy.start()

    def slope_of(x, which):
        pre = dot(x, w2[which])
        sig = 1.0 / (1.0 + jnp.exp(-pre))
        slope[which] = sig * (1.0 + pre * (1.0 - sig))

    slope_of(x_ref[mine], core)
    wt[core] = w2[core].T
    x_copy.wait_recv()
    w_here.wait_recv()
    slope_of(x2[...], 1 - core)
    wt[1 - core] = w2[1 - core].T

    def upper(left, right, dst):
        at = 0
        for i in range(nb):
            prod = dot(left[i * T:(i + 1) * T, :], right[:, i * T:]).astype(bf16)
            for j in range(nb - i):
                dst[(at + j) * T:(at + j + 1) * T, :] = prod[:, j * T:(j + 1) * T]
            at += nb - i

    def act_sum():
        x = jnp.concatenate([x_ref[mine], x_ref[1 - mine]], axis=0)
        xt[...] = x.T
        upper(xt, x, a_own)

    def make_ring(pieces, own, cst, crb, orb, red, xs, xr, sem, xsem):
        each = range(len(pieces))

        def rows_of(chunk, k):
            n, _, first = pieces[k]
            return pl.ds(pl.multiple_of(first + lax.rem(chunk + size, size) * n, 16), n)

        def part(k):
            n, first, _ = pieces[k]
            return slice(first, first + n)

        def slot(k):
            n, first, _ = pieces[k]
            return pl.ds(first, n)

        def copy(kind, src, dst, way, t, k):
            step = (2, 1, 2, 1)[kind]
            return pltpu.make_async_remote_copy(
                src_ref=src, dst_ref=dst,
                send_sem=sem.at[0, kind, way, t, k], recv_sem=sem.at[1, kind, way, t, k],
                device_id=along(step if way == 0 else -step), device_id_type=MESH,
            )

        def sign(way, d):
            return z + d if way == 0 else z - d

        def chain(way, t, k):
            return copy(0, cst.at[way, t, slot(k), :], crb.at[way, t, slot(k), :], way, t, k)

        def odd(way, t, k):
            mine = own.at[rows_of(sign(way, 2 * STAGES - 1 - 2 * t), k), :]
            return copy(1, mine, orb.at[way, t, slot(k), :], way, t, k)

        def spread(kind, way, t, k, chunk):
            there = red.at[rows_of(chunk, k), :]
            return copy(kind, there, there, way, t, k)

        def sent(kind, way, t, k):
            return spread(kind, way, t, k, sign(way, -2 * t))

        def arrived(kind, way, t, k):
            return spread(kind, way, t, k, sign(way, -2 * t - (2, 1)[kind - 2]))

        def across(k):
            return pltpu.make_async_remote_copy(
                src_ref=xs.at[slot(k), :], dst_ref=xr.at[slot(k), :],
                send_sem=xsem.at[0, k], recv_sem=xsem.at[1, k],
                device_id=over, device_id_type=MESH,
            )

        def collect(value, way, t, k, chained):
            odd(way, t, k).wait_recv()
            value = value + orb[way, t, part(k), :].astype(f32)
            if chained:
                chain(way, t, k).wait_recv()
                value = value + crb[way, t, part(k), :].astype(f32)
            return value

        def first(k):
            cst[0, 0, part(k), :] = own[rows_of(z + 2 * STAGES, k), :]
            chain(0, 0, k).start()
            for way in range(2):
                odd(way, 0, k).start()

        def all_first():
            for k in each:
                first(k)

        def middle(t, chained):
            for k in each:
                for way in range(2):
                    odd(way, t, k).start()
            for k in each:
                for way in range(2):
                    value = own[rows_of(sign(way, 2 * STAGES - 2 * t), k), :].astype(f32)
                    value = collect(value, way, t - 1, k, chained[way])
                    cst[way, t, part(k), :] = value.astype(bf16)
                    chain(way, t, k).start()

        def owner():
            for k in each:
                value = own[rows_of(z, k), :].astype(f32)
                for way in range(2):
                    value = collect(value, way, STAGES - 1, k, True)
                xs[part(k), :] = value.astype(bf16)
                across(k).start()

        def start_gather():
            for k in each:
                across(k).wait_recv()
                total = xs[part(k), :].astype(f32) + xr[part(k), :].astype(f32)
                red[rows_of(z, k), :] = total.astype(bf16)
                for kind in (2, 3):
                    for way in range(2):
                        sent(kind, way, 0, k).start()

        def pass_on(t, ways):
            for k in each:
                for way in range(2):
                    arrived(2, way, t - 1, k).wait_recv()
                    if way in ways:
                        sent(2, way, t, k).start()
                    sent(3, way, t, k).start()

        def stage(t, begun=False):
            if not begun:
                pl.when(t == 0)(all_first)
            pl.when(t == 1)(lambda: middle(1, (True, False)))
            pl.when(jnp.logical_and(t > 1, t < STAGES))(lambda: middle(t, (True, True)))
            pl.when(t == STAGES)(owner)
            pl.when(t == STAGES + 1)(start_gather)
            pl.when(jnp.logical_and(t > STAGES + 1, t < 2 * STAGES))(
                lambda: pass_on(t - STAGES - 1, (0, 1))
            )
            pl.when(t == 2 * STAGES)(lambda: pass_on(STAGES - 1, (0,)))

        def finish(k):
            for t in range(STAGES):
                for way in range(2):
                    arrived(3, way, t, k).wait_recv()
            arrived(2, 0, STAGES - 1, k).wait_recv()

        def drain():
            for k in each:
                for way in range(2):
                    def left(t, carry):
                        odd(way, t, k).wait_send()
                        sent(3, way, t, k).wait_send()
                        return carry

                    def left_two(t, carry):
                        chain(way, t + way, k).wait_send()
                        sent(2, way, t, k).wait_send()
                        return carry

                    lax.fori_loop(0, STAGES, left, 0)
                    lax.fori_loop(0, STAGES - way, left_two, 0)
                across(k).wait_send()

        return first, stage, finish, drain

    a_pieces, b_pieces = ring_of(width, size)
    _, a_stage, a_finish, a_drain = make_ring(
        a_pieces, a_own, a_cst, a_crb, a_orb, a_red, a_xs, a_xr, a_sem, a_xsem
    )
    b_first, b_stage, b_finish, b_drain = make_ring(
        b_pieces, b_own, b_cst, b_crb, b_orb, b_red, b_xs, b_xr, b_sem, b_xsem
    )

    ahead = (chips - 1 - chip) * 4 // 7

    def a_ahead(t, carry):
        a_stage(t)
        return carry

    @pl.when(chip < chips - 1)
    def _():
        act_sum()

    lax.fori_loop(0, ahead, a_ahead, 0)

    def chain_copy(r):
        at = pl.ds(pl.multiple_of(r * ROWS, ROWS), ROWS)
        return pltpu.make_async_remote_copy(
            src_ref=dxl.at[0, at, :], dst_ref=dyin.at[at, :],
            send_sem=c_send.at[r], recv_sem=c_recv.at[r],
            device_id=(2 * chip - 1 - core, p), device_id_type=MESH,
        )

    def dh_copy(r):
        at = pl.ds(pl.multiple_of(r * ROWS, ROWS), ROWS)
        return pltpu.make_async_remote_copy(
            src_ref=dhl.at[1 - core, at, :], dst_ref=rdh.at[at, :],
            send_sem=dh_send.at[r], recv_sem=dh_recv.at[r],
            device_id=partner, device_id_type=MESH,
        )

    @pl.when(chip == chips - 1)
    def _():
        get_c.wait()

    def relay(r, carry):
        @pl.when(chip < chips - 1)
        def _():
            chain_copy(r).wait_recv()

        at = pl.ds(pl.multiple_of(r * ROWS, ROWS), ROWS)
        dy = dyin[at, :].astype(f32)
        for which in (1, 0):
            part = (dy * slope[which, at, :]).astype(bf16)
            dhl[which, at, :] = part
            result = (dy + dot(part, wt[which])).astype(bf16)
            dxl[which, at, :] = result
            dy = result.astype(f32)

        @pl.when(chip > 0)
        def _():
            chain_copy(r).start()

        dh_copy(r).start()
        return carry

    lax.fori_loop(0, rows // ROWS, relay, 0)
    dx_copy = pair_copy(dxl.at[1 - core], rdx, 2)
    dx_copy.start()

    @pl.when(chip == chips - 1)
    def _():
        act_sum()

    def dh_wait(r, carry):
        dh_copy(r).wait_recv()
        return carry

    lax.fori_loop(0, rows // ROWS, dh_wait, 0)
    d = jnp.concatenate([dhl[core], rdh[...]], axis=0)
    upper(d.T, d, b_own)
    b_first(0)
    for i in range(nb):
        prod = dot(xt[i * T:(i + 1) * T, :], d).astype(bf16)
        for j in range(nb):
            b_own[tri + (i * nb + j) * T:tri + (i * nb + j + 1) * T, :] = prod[:, j * T:(j + 1) * T]
    b_first(1)

    put_mine = pltpu.make_async_copy(dxl.at[core], dx_ref.at[0, mine], in_sem.at[3])
    put_theirs = pltpu.make_async_copy(rdx, dx_ref.at[0, 1 - mine], in_sem.at[4])

    halves = [slice(h * (width // 2), (h + 1) * (width // 2)) for h in range(2)]

    def newton(src, side, dst):
        at = 0
        squares = jnp.zeros((T, T), f32)
        for i in range(nb):
            for j in range(i, nb):
                block = src[at * T:(at + 1) * T, :].astype(f32) * (1.0 / count)
                if i == j:
                    row = lax.broadcasted_iota(jnp.int32, (T, T), 0)
                    col = lax.broadcasted_iota(jnp.int32, (T, T), 1)
                    block = block + jnp.where(row == col, 0.01, 0.0)
                    squares = squares + block * block
                else:
                    full[j * T:(j + 1) * T, i * T:(i + 1) * T] = block.T
                    squares = squares + 2.0 * (block * block)
                full[i * T:(i + 1) * T, j * T:(j + 1) * T] = block
                at += 1
        scale = 1.0 / jnp.sqrt(jnp.sum(squares, keepdims=True))
        inv[side] = jnp.broadcast_to(scale, inv.shape[1:])
        tb[0] = (full[...] * scale).astype(bf16)
        twice = 2.0 * scale
        for r in halves:
            u = twice * full[r, :] - dot(tb[0, r, :], tb[0])
            ub[0, r, :] = u
            tb[1, r, :] = u.astype(bf16)
        for r in halves:
            v = 2.0 * ub[0, r, :] - dot(tb[1, r, :], tb[1])
            ub[1, r, :] = v
            tb[2, r, :] = v.astype(bf16)
        for r in halves:
            y = twice * full[r, :] + 2.0 * ub[0, r, :] - dot(tb[0, r, :], tb[1])
            last = 4.0 * ub[1, r, :] + 2.0 * y - dot(y.astype(bf16), tb[2])
            dst[r, :] = last.astype(bf16)

    last = 2 * STAGES
    early = ahead >= STAGES

    def both(t, carry):
        b_stage(t, True)

        @pl.when(ahead + t <= last)
        def _():
            a_stage(ahead + t)

        @pl.when(jnp.logical_and(early, t == last - 2))
        def _():
            for k in range(len(a_pieces)):
                a_finish(k)
            newton(a_red, 0, za_ref)

        return carry

    lax.fori_loop(0, last + 1, both, 0)

    @pl.when(jnp.logical_not(early))
    def _():
        for k in range(len(a_pieces)):
            a_finish(k)
        newton(a_red, 0, za_ref)

    dx_copy.wait_recv()
    put_mine.start()
    put_theirs.start()
    b_finish(0)
    newton(b_red, 1, zb)
    b_finish(1)
    scale = inv[0, 0:1, 0:1] * inv[1, 0:1, 0:1]
    for r in halves:
        strips = []
        for i in range(r.start // T, r.stop // T):
            blocks = [tri + (i * nb + j) * T for j in range(nb)]
            strips.append(jnp.concatenate([b_red[at:at + T, :] for at in blocks], axis=1))
        g = jnp.concatenate(strips, axis=0)
        h_ref[r, :] = (8.0 * g.astype(f32) - dot(g, zb[...])) * scale

    def left(r, carry):
        dh_copy(r).wait_send()
        return carry

    lax.fori_loop(0, rows // ROWS, left, 0)

    @pl.when(chip > 0)
    def _():
        def left(r, carry):
            chain_copy(r).wait_send()
            return carry

        lax.fori_loop(0, rows // ROWS, left, 0)

    a_drain()
    b_drain()
    x_copy.wait_send()
    w_copy.wait_send()
    dx_copy.wait_send()
    put_mine.wait()
    put_theirs.wait()


def finish_kernel(dx_ref, h_ref, za_ref, dx_hbm, up_hbm, up, sem):
    put_dx = pltpu.make_async_copy(dx_ref, dx_hbm, sem.at[0])
    put_dx.start()
    h = h_ref[...].astype(jnp.bfloat16)
    puts = []
    for i in range(up.shape[0] // T):
        r = slice(i * T, (i + 1) * T)
        up[r, :] = 8.0 * h_ref[r, :] - dot(za_ref[r, :], h)
        put = pltpu.make_async_copy(up.at[r, :], up_hbm.at[0, r, :], sem.at[1 + i])
        put.start()
        puts.append(put)
    put_dx.wait()
    for put in puts:
        put.wait()


def body(rings, acts, weights, cot_last):
    sections = lax.axis_size("section")
    size = lax.axis_size("dp") // rings
    _, micro, rows, width = acts.shape
    vmem = pl.BlockSpec(memory_space=pltpu.VMEM)
    hbm = pl.BlockSpec(memory_space=pltpu.HBM)
    bf16, f32 = jnp.bfloat16, jnp.float32
    dma = pltpu.SemaphoreType.DMA

    def ring_scratch(pieces):
        piece = sum(n for n, _, _ in pieces)
        passing = pltpu.VMEM((2, STAGES, piece, T), bf16)
        whole = pltpu.VMEM((piece * size, T), bf16)
        message = pltpu.VMEM((piece, T), bf16)
        return [whole, passing, passing, passing, whole, message, message]

    a_pieces, b_pieces = ring_of(width, size)
    dx, h, za = pl.pallas_call(
        functools.partial(kernel, sections, rings, size),
        name="relay",
        out_shape=(
            jax.ShapeDtypeStruct((1, micro, rows, width), bf16),
            jax.ShapeDtypeStruct((width, width), f32),
            jax.ShapeDtypeStruct((width, width), bf16),
        ),
        in_specs=[hbm] * 3,
        out_specs=(vmem, vmem, vmem),
        scratch_shapes=[
            pltpu.VMEM((micro, rows, width), bf16),
            pltpu.VMEM((2, width, width), bf16),
            pltpu.VMEM((2, width, width), bf16),
            pltpu.VMEM((rows, width), bf16),
            pltpu.VMEM((2, rows, width), f32),
            pltpu.VMEM((width, micro * rows), bf16),
            pltpu.VMEM((rows, width), bf16),
            pltpu.VMEM((2, rows, width), bf16),
            pltpu.VMEM((2, rows, width), bf16),
            pltpu.VMEM((rows, width), bf16),
            pltpu.VMEM((rows, width), bf16),
            *ring_scratch(a_pieces),
            *ring_scratch(b_pieces),
            pltpu.VMEM((width, width), f32),
            pltpu.VMEM((3, width, width), bf16),
            pltpu.VMEM((2, width, width), f32),
            pltpu.VMEM((width, width), bf16),
            pltpu.VMEM((2, 8, T), f32),
            dma((5,)), dma((2, 3)),
            dma((rows // ROWS,)), dma((rows // ROWS,)),
            dma((rows // ROWS,)), dma((rows // ROWS,)),
            dma((2, 4, 2, STAGES, len(a_pieces))), dma((2, len(a_pieces))),
            dma((2, 4, 2, STAGES, len(b_pieces))), dma((2, len(b_pieces))),
        ],
        compiler_params=pltpu.CompilerParams(
            collective_id=0, has_side_effects=True, vmem_limit_bytes=48 << 20
        ),
    )(*(pltpu.with_memory_space_constraint(a, pltpu.HBM) for a in (acts, weights, cot_last)))
    return pl.pallas_call(
        finish_kernel,
        name="finish",
        out_shape=(
            jax.ShapeDtypeStruct((1, micro, rows, width), bf16),
            jax.ShapeDtypeStruct((1, width, width), f32),
        ),
        in_specs=[vmem] * 3,
        out_specs=(hbm, hbm),
        scratch_shapes=[
            pltpu.VMEM((width, width), f32),
            dma((1 + width // T,)),
        ],
        compiler_params=pltpu.CompilerParams(vmem_limit_bytes=8 << 20),
    )(dx, h, za)


def solution(mesh):
    placed = (P("section", None, "dp", None), P("section", None, None), P(None, "dp", None))
    return jax.shard_map(
        functools.partial(body, 2),
        mesh=mesh,
        in_specs=placed,
        out_specs=(P("section", None, "dp", None), P("section", None, None)),
        check_vma=False,
    )
```

```python
import functools

import jax
import jax.numpy as jnp
from jax import lax
from jax.experimental import pallas as pl
from jax.experimental.pallas import tpu as pltpu
from jax.sharding import PartitionSpec as P

MESH = pl.DeviceIdType.MESH
T = 128
ROWS = 16
STAGES = 4


def dot(a, b):
    return jnp.dot(a, b, preferred_element_type=jnp.float32)


def ring_of(width, size):
    nb = width // T
    tri, square = nb * (nb + 1) // 2 * T, nb * nb * T
    o, g = tri // size, square // size
    return ((o, 0, 0),), ((o, 0, 0), (g, o, tri))


def kernel(
    sections, rings, size,
    acts_hbm, w_hbm, cot_hbm, dx_ref, h_ref, za_ref,
    x_ref, w2, wt, x2, slope, xt, dyin, dhl, dxl, rdh, rdx,
    a_own, a_cst, a_crb, a_orb, a_red, a_xs, a_xr,
    b_own, b_cst, b_crb, b_orb, b_red, b_xs, b_xr,
    full, tb, ub, zb, inv,
    in_sem, pair_sem, dh_send, dh_recv, c_send, c_recv,
    a_sem, a_xsem, b_sem, b_xsem,
):
    s = lax.axis_index("section")
    p = lax.axis_index("dp")
    z, ring = lax.rem(p, size), p // size
    base = ring * size
    core, chip = lax.rem(s, 2), s // 2
    chips = sections // 2
    mine = lax.rem(core + chips - 1 - chip, 2)
    width = w2.shape[1]
    nb = width // T
    tri = nb * (nb + 1) // 2 * T
    rows = dyin.shape[0]
    micro = x_ref.shape[0]
    count = micro * rows * rings * size
    f32, bf16 = jnp.float32, jnp.bfloat16

    def along(d):
        return (s, base + lax.rem(z + size + d, size))

    over = (s, lax.rem(p + size, rings * size))
    partner = (s + 1 - 2 * core, p)

    barrier = pltpu.get_barrier_semaphore()
    peers = (along(1), along(-1), along(2), along(-2), over, partner, (2 * lax.rem(chip + 1, chips) + 1 - core, p))
    for peer in peers:
        pl.semaphore_signal(barrier, inc=1, device_id=peer, device_id_type=MESH)

    get_x = pltpu.make_async_copy(acts_hbm.at[0], x_ref, in_sem.at[0])
    get_w = pltpu.make_async_copy(w_hbm.at[0], w2.at[core], in_sem.at[1])
    get_c = pltpu.make_async_copy(cot_hbm.at[mine], dyin, in_sem.at[2])
    get_x.start()
    get_w.start()

    @pl.when(chip == chips - 1)
    def _():
        get_c.start()

    get_x.wait()
    get_w.wait()
    pl.semaphore_wait(barrier, len(peers))

    def pair_copy(src, dst, i):
        return pltpu.make_async_remote_copy(
            src_ref=src, dst_ref=dst, send_sem=pair_sem.at[0, i], recv_sem=pair_sem.at[1, i],
            device_id=partner, device_id_type=MESH,
        )

    x_copy = pair_copy(x_ref.at[1 - mine], x2, 0)
    w_copy = pair_copy(w2.at[core], w2.at[core], 1)
    w_here = pair_copy(w2.at[1 - core], w2.at[1 - core], 1)
    x_copy.start()
    w_copy.start()

    def slope_of(x, which):
        pre = dot(x, w2[which])
        sig = 1.0 / (1.0 + jnp.exp(-pre))
        slope[which] = sig * (1.0 + pre * (1.0 - sig))

    slope_of(x_ref[mine], core)
    wt[core] = w2[core].T
    x_copy.wait_recv()
    w_here.wait_recv()
    slope_of(x2[...], 1 - core)
    wt[1 - core] = w2[1 - core].T

    def upper(left, right, dst):
        at = 0
        for i in range(nb):
            prod = dot(left[i * T:(i + 1) * T, :], right[:, i * T:]).astype(bf16)
            for j in range(nb - i):
                dst[(at + j) * T:(at + j + 1) * T, :] = prod[:, j * T:(j + 1) * T]
            at += nb - i

    def act_sum():
        x = jnp.concatenate([x_ref[mine], x_ref[1 - mine]], axis=0)
        xt[...] = x.T
        upper(xt, x, a_own)

    def make_ring(pieces, own, cst, crb, orb, red, xs, xr, sem, xsem):
        each = range(len(pieces))

        def rows_of(chunk, k):
            n, _, first = pieces[k]
            return pl.ds(pl.multiple_of(first + lax.rem(chunk + size, size) * n, 16), n)

        def part(k):
            n, first, _ = pieces[k]
            return slice(first, first + n)

        def slot(k):
            n, first, _ = pieces[k]
            return pl.ds(first, n)

        def copy(kind, src, dst, way, t, k):
            step = (2, 1, 2, 1)[kind]
            return pltpu.make_async_remote_copy(
                src_ref=src, dst_ref=dst,
                send_sem=sem.at[0, kind, way, t, k], recv_sem=sem.at[1, kind, way, t, k],
                device_id=along(step if way == 0 else -step), device_id_type=MESH,
            )

        def sign(way, d):
            return z + d if way == 0 else z - d

        def chain(way, t, k):
            return copy(0, cst.at[way, t, slot(k), :], crb.at[way, t, slot(k), :], way, t, k)

        def odd(way, t, k):
            mine = own.at[rows_of(sign(way, 2 * STAGES - 1 - 2 * t), k), :]
            return copy(1, mine, orb.at[way, t, slot(k), :], way, t, k)

        def spread(kind, way, t, k, chunk):
            there = red.at[rows_of(chunk, k), :]
            return copy(kind, there, there, way, t, k)

        def sent(kind, way, t, k):
            return spread(kind, way, t, k, sign(way, -2 * t))

        def arrived(kind, way, t, k):
            return spread(kind, way, t, k, sign(way, -2 * t - (2, 1)[kind - 2]))

        def across(k):
            return pltpu.make_async_remote_copy(
                src_ref=xs.at[slot(k), :], dst_ref=xr.at[slot(k), :],
                send_sem=xsem.at[0, k], recv_sem=xsem.at[1, k],
                device_id=over, device_id_type=MESH,
            )

        def collect(value, way, t, k, chained):
            odd(way, t, k).wait_recv()
            value = value + orb[way, t, part(k), :].astype(f32)
            if chained:
                chain(way, t, k).wait_recv()
                value = value + crb[way, t, part(k), :].astype(f32)
            return value

        def first(k):
            cst[0, 0, part(k), :] = own[rows_of(z + 2 * STAGES, k), :]
            chain(0, 0, k).start()
            for way in range(2):
                odd(way, 0, k).start()

        def all_first():
            for k in each:
                first(k)

        def middle(t, chained):
            for k in each:
                for way in range(2):
                    odd(way, t, k).start()
            for k in each:
                for way in range(2):
                    value = own[rows_of(sign(way, 2 * STAGES - 2 * t), k), :].astype(f32)
                    value = collect(value, way, t - 1, k, chained[way])
                    cst[way, t, part(k), :] = value.astype(bf16)
                    chain(way, t, k).start()

        def owner():
            for k in each:
                value = own[rows_of(z, k), :].astype(f32)
                for way in range(2):
                    value = collect(value, way, STAGES - 1, k, True)
                xs[part(k), :] = value.astype(bf16)
                across(k).start()

        def start_gather():
            for k in each:
                across(k).wait_recv()
                total = xs[part(k), :].astype(f32) + xr[part(k), :].astype(f32)
                red[rows_of(z, k), :] = total.astype(bf16)
                for kind in (2, 3):
                    for way in range(2):
                        sent(kind, way, 0, k).start()

        def pass_on(t, ways):
            for k in each:
                for way in range(2):
                    arrived(2, way, t - 1, k).wait_recv()
                    if way in ways:
                        sent(2, way, t, k).start()
                    sent(3, way, t, k).start()

        def stage(t, begun=False):
            if not begun:
                pl.when(t == 0)(all_first)
            pl.when(t == 1)(lambda: middle(1, (True, False)))
            pl.when(jnp.logical_and(t > 1, t < STAGES))(lambda: middle(t, (True, True)))
            pl.when(t == STAGES)(owner)
            pl.when(t == STAGES + 1)(start_gather)
            pl.when(jnp.logical_and(t > STAGES + 1, t < 2 * STAGES))(
                lambda: pass_on(t - STAGES - 1, (0, 1))
            )
            pl.when(t == 2 * STAGES)(lambda: pass_on(STAGES - 1, (0,)))

        def finish(k):
            for t in range(STAGES):
                for way in range(2):
                    arrived(3, way, t, k).wait_recv()
            arrived(2, 0, STAGES - 1, k).wait_recv()

        def drain():
            for k in each:
                for way in range(2):
                    def left(t, carry):
                        odd(way, t, k).wait_send()
                        sent(3, way, t, k).wait_send()
                        return carry

                    def left_two(t, carry):
                        chain(way, t + way, k).wait_send()
                        sent(2, way, t, k).wait_send()
                        return carry

                    lax.fori_loop(0, STAGES, left, 0)
                    lax.fori_loop(0, STAGES - way, left_two, 0)
                across(k).wait_send()

        return first, stage, finish, drain

    a_pieces, b_pieces = ring_of(width, size)
    _, a_stage, a_finish, a_drain = make_ring(
        a_pieces, a_own, a_cst, a_crb, a_orb, a_red, a_xs, a_xr, a_sem, a_xsem
    )
    b_first, b_stage, b_finish, b_drain = make_ring(
        b_pieces, b_own, b_cst, b_crb, b_orb, b_red, b_xs, b_xr, b_sem, b_xsem
    )

    ahead = (chips - 1 - chip) * 4 // 7

    def a_ahead(t, carry):
        a_stage(t)
        return carry

    @pl.when(chip < chips - 1)
    def _():
        act_sum()

    lax.fori_loop(0, ahead, a_ahead, 0)

    def chain_copy(r):
        at = pl.ds(pl.multiple_of(r * ROWS, ROWS), ROWS)
        return pltpu.make_async_remote_copy(
            src_ref=dxl.at[0, at, :], dst_ref=dyin.at[at, :],
            send_sem=c_send.at[r], recv_sem=c_recv.at[r],
            device_id=(2 * chip - 1 - core, p), device_id_type=MESH,
        )

    def dh_copy(r):
        at = pl.ds(pl.multiple_of(r * ROWS, ROWS), ROWS)
        return pltpu.make_async_remote_copy(
            src_ref=dhl.at[1 - core, at, :], dst_ref=rdh.at[at, :],
            send_sem=dh_send.at[r], recv_sem=dh_recv.at[r],
            device_id=partner, device_id_type=MESH,
        )

    @pl.when(chip == chips - 1)
    def _():
        get_c.wait()

    def relay(r, carry):
        @pl.when(chip < chips - 1)
        def _():
            chain_copy(r).wait_recv()

        at = pl.ds(pl.multiple_of(r * ROWS, ROWS), ROWS)
        dy = dyin[at, :].astype(f32)
        for which in (1, 0):
            part = (dy * slope[which, at, :]).astype(bf16)
            dhl[which, at, :] = part
            result = (dy + dot(part, wt[which])).astype(bf16)
            dxl[which, at, :] = result
            dy = result.astype(f32)

        @pl.when(chip > 0)
        def _():
            chain_copy(r).start()

        dh_copy(r).start()
        return carry

    lax.fori_loop(0, rows // ROWS, relay, 0)
    dx_copy = pair_copy(dxl.at[1 - core], rdx, 2)
    dx_copy.start()

    @pl.when(chip == chips - 1)
    def _():
        act_sum()

    def dh_wait(r, carry):
        dh_copy(r).wait_recv()
        return carry

    lax.fori_loop(0, rows // ROWS, dh_wait, 0)
    d = jnp.concatenate([dhl[core], rdh[...]], axis=0)
    upper(d.T, d, b_own)
    b_first(0)
    for i in range(nb):
        prod = dot(xt[i * T:(i + 1) * T, :], d).astype(bf16)
        for j in range(nb):
            b_own[tri + (i * nb + j) * T:tri + (i * nb + j + 1) * T, :] = prod[:, j * T:(j + 1) * T]
    b_first(1)

    put_mine = pltpu.make_async_copy(dxl.at[core], dx_ref.at[0, mine], in_sem.at[3])
    put_theirs = pltpu.make_async_copy(rdx, dx_ref.at[0, 1 - mine], in_sem.at[4])

    halves = [slice(h * (width // 2), (h + 1) * (width // 2)) for h in range(2)]

    def newton(src, side, dst):
        at = 0
        squares = jnp.zeros((T, T), f32)
        for i in range(nb):
            for j in range(i, nb):
                block = src[at * T:(at + 1) * T, :].astype(f32) * (1.0 / count)
                if i == j:
                    row = lax.broadcasted_iota(jnp.int32, (T, T), 0)
                    col = lax.broadcasted_iota(jnp.int32, (T, T), 1)
                    block = block + jnp.where(row == col, 0.01, 0.0)
                    squares = squares + block * block
                else:
                    full[j * T:(j + 1) * T, i * T:(i + 1) * T] = block.T
                    squares = squares + 2.0 * (block * block)
                full[i * T:(i + 1) * T, j * T:(j + 1) * T] = block
                at += 1
        scale = 1.0 / jnp.sqrt(jnp.sum(squares, keepdims=True))
        inv[side] = jnp.broadcast_to(scale, inv.shape[1:])
        tb[0] = (full[...] * scale).astype(bf16)
        twice = 2.0 * scale
        for r in halves:
            u = twice * full[r, :] - dot(tb[0, r, :], tb[0])
            ub[0, r, :] = u
            tb[1, r, :] = u.astype(bf16)
        for r in halves:
            v = 2.0 * ub[0, r, :] - dot(tb[1, r, :], tb[1])
            ub[1, r, :] = v
            tb[2, r, :] = v.astype(bf16)
        for r in halves:
            y = twice * full[r, :] + 2.0 * ub[0, r, :] - dot(tb[0, r, :], tb[1])
            last = 4.0 * ub[1, r, :] + 2.0 * y - dot(y.astype(bf16), tb[2])
            dst[r, :] = last.astype(bf16)

    last = 2 * STAGES
    early = ahead >= STAGES

    def both(t, carry):
        b_stage(t, True)

        @pl.when(ahead + t <= last)
        def _():
            a_stage(ahead + t)

        @pl.when(jnp.logical_and(early, t == last - 2))
        def _():
            for k in range(len(a_pieces)):
                a_finish(k)
            newton(a_red, 0, za_ref)

        return carry

    lax.fori_loop(0, last + 1, both, 0)

    @pl.when(jnp.logical_not(early))
    def _():
        for k in range(len(a_pieces)):
            a_finish(k)
        newton(a_red, 0, za_ref)

    dx_copy.wait_recv()
    put_mine.start()
    put_theirs.start()
    def left(r, carry):
        dh_copy(r).wait_send()
        return carry

    lax.fori_loop(0, rows // ROWS, left, 0)

    @pl.when(chip > 0)
    def _():
        def left(r, carry):
            chain_copy(r).wait_send()
            return carry

        lax.fori_loop(0, rows // ROWS, left, 0)

    a_drain()
    b_drain()
    x_copy.wait_send()
    w_copy.wait_send()
    dx_copy.wait_send()

    b_finish(0)
    newton(b_red, 1, zb)
    b_finish(1)
    scale = inv[0, 0:1, 0:1] * inv[1, 0:1, 0:1]
    for r in halves:
        strips = []
        for i in range(r.start // T, r.stop // T):
            blocks = [tri + (i * nb + j) * T for j in range(nb)]
            strips.append(jnp.concatenate([b_red[at:at + T, :] for at in blocks], axis=1))
        g = jnp.concatenate(strips, axis=0)
        h_ref[r, :] = (8.0 * g.astype(f32) - dot(g, zb[...])) * scale

    put_mine.wait()
    put_theirs.wait()


def finish_kernel(dx_ref, h_ref, za_ref, dx_hbm, up_hbm, up, sem):
    put_dx = pltpu.make_async_copy(dx_ref, dx_hbm, sem.at[0])
    put_dx.start()
    h = h_ref[...].astype(jnp.bfloat16)
    puts = []
    for i in range(up.shape[0] // T):
        r = slice(i * T, (i + 1) * T)
        up[r, :] = 8.0 * h_ref[r, :] - dot(za_ref[r, :], h)
        put = pltpu.make_async_copy(up.at[r, :], up_hbm.at[0, r, :], sem.at[1 + i])
        put.start()
        puts.append(put)
    put_dx.wait()
    for put in puts:
        put.wait()


def body(rings, acts, weights, cot_last):
    sections = lax.axis_size("section")
    size = lax.axis_size("dp") // rings
    _, micro, rows, width = acts.shape
    vmem = pl.BlockSpec(memory_space=pltpu.VMEM)
    hbm = pl.BlockSpec(memory_space=pltpu.HBM)
    bf16, f32 = jnp.bfloat16, jnp.float32
    dma = pltpu.SemaphoreType.DMA

    def ring_scratch(pieces):
        piece = sum(n for n, _, _ in pieces)
        passing = pltpu.VMEM((2, STAGES, piece, T), bf16)
        whole = pltpu.VMEM((piece * size, T), bf16)
        message = pltpu.VMEM((piece, T), bf16)
        return [whole, passing, passing, passing, whole, message, message]

    a_pieces, b_pieces = ring_of(width, size)
    dx, h, za = pl.pallas_call(
        functools.partial(kernel, sections, rings, size),
        name="relay",
        out_shape=(
            jax.ShapeDtypeStruct((1, micro, rows, width), bf16),
            jax.ShapeDtypeStruct((width, width), f32),
            jax.ShapeDtypeStruct((width, width), bf16),
        ),
        in_specs=[hbm] * 3,
        out_specs=(vmem, vmem, vmem),
        scratch_shapes=[
            pltpu.VMEM((micro, rows, width), bf16),
            pltpu.VMEM((2, width, width), bf16),
            pltpu.VMEM((2, width, width), bf16),
            pltpu.VMEM((rows, width), bf16),
            pltpu.VMEM((2, rows, width), f32),
            pltpu.VMEM((width, micro * rows), bf16),
            pltpu.VMEM((rows, width), bf16),
            pltpu.VMEM((2, rows, width), bf16),
            pltpu.VMEM((2, rows, width), bf16),
            pltpu.VMEM((rows, width), bf16),
            pltpu.VMEM((rows, width), bf16),
            *ring_scratch(a_pieces),
            *ring_scratch(b_pieces),
            pltpu.VMEM((width, width), f32),
            pltpu.VMEM((3, width, width), bf16),
            pltpu.VMEM((2, width, width), f32),
            pltpu.VMEM((width, width), bf16),
            pltpu.VMEM((2, 8, T), f32),
            dma((5,)), dma((2, 3)),
            dma((rows // ROWS,)), dma((rows // ROWS,)),
            dma((rows // ROWS,)), dma((rows // ROWS,)),
            dma((2, 4, 2, STAGES, len(a_pieces))), dma((2, len(a_pieces))),
            dma((2, 4, 2, STAGES, len(b_pieces))), dma((2, len(b_pieces))),
        ],
        compiler_params=pltpu.CompilerParams(
            collective_id=0, has_side_effects=True, vmem_limit_bytes=48 << 20
        ),
    )(*(pltpu.with_memory_space_constraint(a, pltpu.HBM) for a in (acts, weights, cot_last)))
    return pl.pallas_call(
        finish_kernel,
        name="finish",
        out_shape=(
            jax.ShapeDtypeStruct((1, micro, rows, width), bf16),
            jax.ShapeDtypeStruct((1, width, width), f32),
        ),
        in_specs=[vmem] * 3,
        out_specs=(hbm, hbm),
        scratch_shapes=[
            pltpu.VMEM((width, width), f32),
            dma((1 + width // T,)),
        ],
        compiler_params=pltpu.CompilerParams(vmem_limit_bytes=8 << 20),
    )(dx, h, za)


def solution(mesh):
    placed = (P("section", None, "dp", None), P("section", None, None), P(None, "dp", None))
    return jax.shard_map(
        functools.partial(body, 2),
        mesh=mesh,
        in_specs=placed,
        out_specs=(P("section", None, "dp", None), P("section", None, None)),
        check_vma=False,
    )
```

```python
import functools

import jax
import jax.numpy as jnp
from jax import lax
from jax.experimental import pallas as pl
from jax.experimental.pallas import tpu as pltpu
from jax.sharding import PartitionSpec as P

MESH = pl.DeviceIdType.MESH
T = 128
ROWS = 16
STAGES = 4


def dot(a, b):
    return jnp.dot(a, b, preferred_element_type=jnp.float32)


def ring_of(width, size):
    nb = width // T
    tri, square = nb * (nb + 1) // 2 * T, nb * nb * T
    o, g = tri // size, square // size
    return ((o, 0, 0),), ((o, 0, 0), (g, o, tri))


def kernel(
    sections, rings, size,
    acts_hbm, w_hbm, cot_hbm, dx_ref, h_ref, za_ref,
    x_ref, w2, wt, x2, slope, xt, dyin, dhl, dxl, rdh, rdx,
    a_own, a_cst, a_crb, a_orb, a_red, a_xs, a_xr,
    b_own, b_cst, b_crb, b_orb, b_red, b_xs, b_xr,
    full, tb, ub, zb, inv,
    in_sem, pair_sem, dh_send, dh_recv, c_send, c_recv,
    a_sem, a_xsem, b_sem, b_xsem,
):
    s = lax.axis_index("section")
    p = lax.axis_index("dp")
    z, ring = lax.rem(p, size), p // size
    base = ring * size
    core, chip = lax.rem(s, 2), s // 2
    chips = sections // 2
    mine = lax.rem(core + chips - 1 - chip, 2)
    width = w2.shape[1]
    nb = width // T
    tri = nb * (nb + 1) // 2 * T
    rows = dyin.shape[0]
    micro = x_ref.shape[0]
    count = micro * rows * rings * size
    f32, bf16 = jnp.float32, jnp.bfloat16

    def along(d):
        return (s, base + lax.rem(z + size + d, size))

    over = (s, lax.rem(p + size, rings * size))
    partner = (s + 1 - 2 * core, p)

    barrier = pltpu.get_barrier_semaphore()
    peers = (along(1), along(-1), along(2), along(-2), over, partner, (2 * lax.rem(chip + 1, chips) + 1 - core, p))
    for peer in peers:
        pl.semaphore_signal(barrier, inc=1, device_id=peer, device_id_type=MESH)

    get_x = pltpu.make_async_copy(acts_hbm.at[0], x_ref, in_sem.at[0])
    get_w = pltpu.make_async_copy(w_hbm.at[0], w2.at[core], in_sem.at[1])
    get_c = pltpu.make_async_copy(cot_hbm.at[mine], dyin, in_sem.at[2])
    get_x.start()
    get_w.start()

    @pl.when(chip == chips - 1)
    def _():
        get_c.start()

    get_x.wait()
    get_w.wait()
    pl.semaphore_wait(barrier, len(peers))

    def pair_copy(src, dst, i):
        return pltpu.make_async_remote_copy(
            src_ref=src, dst_ref=dst, send_sem=pair_sem.at[0, i], recv_sem=pair_sem.at[1, i],
            device_id=partner, device_id_type=MESH,
        )

    x_copy = pair_copy(x_ref.at[1 - mine], x2, 0)
    w_copy = pair_copy(w2.at[core], w2.at[core], 1)
    w_here = pair_copy(w2.at[1 - core], w2.at[1 - core], 1)
    x_copy.start()
    w_copy.start()

    def slope_of(x, which):
        pre = dot(x, w2[which])
        sig = 1.0 / (1.0 + jnp.exp(-pre))
        slope[which] = sig * (1.0 + pre * (1.0 - sig))

    slope_of(x_ref[mine], core)
    wt[core] = w2[core].T
    x_copy.wait_recv()
    w_here.wait_recv()
    slope_of(x2[...], 1 - core)
    wt[1 - core] = w2[1 - core].T

    def upper(left, right, dst):
        at = 0
        for i in range(nb):
            prod = dot(left[i * T:(i + 1) * T, :], right[:, i * T:]).astype(bf16)
            for j in range(nb - i):
                dst[(at + j) * T:(at + j + 1) * T, :] = prod[:, j * T:(j + 1) * T]
            at += nb - i

    def act_sum():
        x = jnp.concatenate([x_ref[mine], x_ref[1 - mine]], axis=0)
        xt[...] = x.T
        upper(xt, x, a_own)

    def make_ring(pieces, own, cst, crb, orb, red, xs, xr, sem, xsem):
        each = range(len(pieces))

        def rows_of(chunk, k):
            n, _, first = pieces[k]
            return pl.ds(pl.multiple_of(first + lax.rem(chunk + size, size) * n, 16), n)

        def part(k):
            n, first, _ = pieces[k]
            return slice(first, first + n)

        def slot(k):
            n, first, _ = pieces[k]
            return pl.ds(first, n)

        def copy(kind, src, dst, way, t, k):
            step = (2, 1, 2, 1)[kind]
            return pltpu.make_async_remote_copy(
                src_ref=src, dst_ref=dst,
                send_sem=sem.at[0, kind, way, t, k], recv_sem=sem.at[1, kind, way, t, k],
                device_id=along(step if way == 0 else -step), device_id_type=MESH,
            )

        def sign(way, d):
            return z + d if way == 0 else z - d

        def chain(way, t, k):
            return copy(0, cst.at[way, t, slot(k), :], crb.at[way, t, slot(k), :], way, t, k)

        def odd(way, t, k):
            mine = own.at[rows_of(sign(way, 2 * STAGES - 1 - 2 * t), k), :]
            return copy(1, mine, orb.at[way, t, slot(k), :], way, t, k)

        def spread(kind, way, t, k, chunk):
            there = red.at[rows_of(chunk, k), :]
            return copy(kind, there, there, way, t, k)

        def sent(kind, way, t, k):
            return spread(kind, way, t, k, sign(way, -2 * t))

        def arrived(kind, way, t, k):
            return spread(kind, way, t, k, sign(way, -2 * t - (2, 1)[kind - 2]))

        def across(k):
            return pltpu.make_async_remote_copy(
                src_ref=xs.at[slot(k), :], dst_ref=xr.at[slot(k), :],
                send_sem=xsem.at[0, k], recv_sem=xsem.at[1, k],
                device_id=over, device_id_type=MESH,
            )

        def collect(value, way, t, k, chained):
            odd(way, t, k).wait_recv()
            value = value + orb[way, t, part(k), :].astype(f32)
            if chained:
                chain(way, t, k).wait_recv()
                value = value + crb[way, t, part(k), :].astype(f32)
            return value

        def first(k):
            cst[0, 0, part(k), :] = own[rows_of(z + 2 * STAGES, k), :]
            chain(0, 0, k).start()
            for way in range(2):
                odd(way, 0, k).start()

        def all_first():
            for k in each:
                first(k)

        def middle(t, chained):
            for k in each:
                for way in range(2):
                    odd(way, t, k).start()
            for k in each:
                for way in range(2):
                    value = own[rows_of(sign(way, 2 * STAGES - 2 * t), k), :].astype(f32)
                    value = collect(value, way, t - 1, k, chained[way])
                    cst[way, t, part(k), :] = value.astype(bf16)
                    chain(way, t, k).start()

        def owner():
            for k in each:
                value = own[rows_of(z, k), :].astype(f32)
                for way in range(2):
                    value = collect(value, way, STAGES - 1, k, True)
                xs[part(k), :] = value.astype(bf16)
                across(k).start()

        def start_gather():
            for k in each:
                across(k).wait_recv()
                total = xs[part(k), :].astype(f32) + xr[part(k), :].astype(f32)
                red[rows_of(z, k), :] = total.astype(bf16)
                for kind in (2, 3):
                    for way in range(2):
                        sent(kind, way, 0, k).start()

        def pass_on(t, ways):
            for k in each:
                for way in range(2):
                    arrived(2, way, t - 1, k).wait_recv()
                    if way in ways:
                        sent(2, way, t, k).start()
                    sent(3, way, t, k).start()

        def stage(t, begun=False):
            if not begun:
                pl.when(t == 0)(all_first)
            pl.when(t == 1)(lambda: middle(1, (True, False)))
            pl.when(jnp.logical_and(t > 1, t < STAGES))(lambda: middle(t, (True, True)))
            pl.when(t == STAGES)(owner)
            pl.when(t == STAGES + 1)(start_gather)
            pl.when(jnp.logical_and(t > STAGES + 1, t < 2 * STAGES))(
                lambda: pass_on(t - STAGES - 1, (0, 1))
            )
            pl.when(t == 2 * STAGES)(lambda: pass_on(STAGES - 1, (0,)))

        def finish(k):
            for t in range(STAGES):
                for way in range(2):
                    arrived(3, way, t, k).wait_recv()
            arrived(2, 0, STAGES - 1, k).wait_recv()

        def drain():
            for k in each:
                for way in range(2):
                    def left(t, carry):
                        odd(way, t, k).wait_send()
                        sent(3, way, t, k).wait_send()
                        return carry

                    def left_two(t, carry):
                        chain(way, t + way, k).wait_send()
                        sent(2, way, t, k).wait_send()
                        return carry

                    lax.fori_loop(0, STAGES, left, 0)
                    lax.fori_loop(0, STAGES - way, left_two, 0)
                across(k).wait_send()

        return first, stage, finish, drain

    a_pieces, b_pieces = ring_of(width, size)
    _, a_stage, a_finish, a_drain = make_ring(
        a_pieces, a_own, a_cst, a_crb, a_orb, a_red, a_xs, a_xr, a_sem, a_xsem
    )
    b_first, b_stage, b_finish, b_drain = make_ring(
        b_pieces, b_own, b_cst, b_crb, b_orb, b_red, b_xs, b_xr, b_sem, b_xsem
    )

    ahead = (chips - 1 - chip) * 4 // 7

    def a_ahead(t, carry):
        a_stage(t)
        return carry

    @pl.when(chip < chips - 1)
    def _():
        act_sum()

    lax.fori_loop(0, ahead, a_ahead, 0)

    def chain_copy(r):
        at = pl.ds(pl.multiple_of(r * ROWS, ROWS), ROWS)
        return pltpu.make_async_remote_copy(
            src_ref=dxl.at[0, at, :], dst_ref=dyin.at[at, :],
            send_sem=c_send.at[r], recv_sem=c_recv.at[r],
            device_id=(lax.rem(2 * chip + sections - 1 - core, sections), p),
            device_id_type=MESH,
        )

    def dh_copy(r):
        at = pl.ds(pl.multiple_of(r * ROWS, ROWS), ROWS)
        return pltpu.make_async_remote_copy(
            src_ref=dhl.at[1 - core, at, :], dst_ref=rdh.at[at, :],
            send_sem=dh_send.at[r], recv_sem=dh_recv.at[r],
            device_id=partner, device_id_type=MESH,
        )

    @pl.when(chip == chips - 1)
    def _():
        get_c.wait()

    def relay(r, carry):
        @pl.when(chip < chips - 1)
        def _():
            chain_copy(r).wait_recv()

        at = pl.ds(pl.multiple_of(r * ROWS, ROWS), ROWS)
        dy = dyin[at, :].astype(f32)
        for which in (1, 0):
            part = (dy * slope[which, at, :]).astype(bf16)
            dhl[which, at, :] = part
            result = (dy + dot(part, wt[which])).astype(bf16)
            dxl[which, at, :] = result
            dy = result.astype(f32)

        @pl.when(chip > 0)
        def _():
            chain_copy(r).start()

        dh_copy(r).start()
        return carry

    lax.fori_loop(0, rows // ROWS, relay, 0)
    dx_copy = pair_copy(dxl.at[1 - core], rdx, 2)
    dx_copy.start()

    @pl.when(chip == chips - 1)
    def _():
        act_sum()

    def dh_wait(r, carry):
        dh_copy(r).wait_recv()
        return carry

    lax.fori_loop(0, rows // ROWS, dh_wait, 0)
    d = jnp.concatenate([dhl[core], rdh[...]], axis=0)
    upper(d.T, d, b_own)
    b_first(0)
    for i in range(nb):
        prod = dot(xt[i * T:(i + 1) * T, :], d).astype(bf16)
        for j in range(nb):
            b_own[tri + (i * nb + j) * T:tri + (i * nb + j + 1) * T, :] = prod[:, j * T:(j + 1) * T]
    b_first(1)

    put_mine = pltpu.make_async_copy(dxl.at[core], dx_ref.at[0, mine], in_sem.at[3])
    put_theirs = pltpu.make_async_copy(rdx, dx_ref.at[0, 1 - mine], in_sem.at[4])

    halves = [slice(h * (width // 2), (h + 1) * (width // 2)) for h in range(2)]

    def newton(src, side, dst):
        at = 0
        squares = jnp.zeros((T, T), f32)
        for i in range(nb):
            for j in range(i, nb):
                block = src[at * T:(at + 1) * T, :].astype(f32) * (1.0 / count)
                if i == j:
                    row = lax.broadcasted_iota(jnp.int32, (T, T), 0)
                    col = lax.broadcasted_iota(jnp.int32, (T, T), 1)
                    block = block + jnp.where(row == col, 0.01, 0.0)
                    squares = squares + block * block
                else:
                    full[j * T:(j + 1) * T, i * T:(i + 1) * T] = block.T
                    squares = squares + 2.0 * (block * block)
                full[i * T:(i + 1) * T, j * T:(j + 1) * T] = block
                at += 1
        scale = 1.0 / jnp.sqrt(jnp.sum(squares, keepdims=True))
        inv[side] = jnp.broadcast_to(scale, inv.shape[1:])
        tb[0] = (full[...] * scale).astype(bf16)
        twice = 2.0 * scale
        for r in halves:
            u = twice * full[r, :] - dot(tb[0, r, :], tb[0])
            ub[0, r, :] = u
            tb[1, r, :] = u.astype(bf16)
        for r in halves:
            v = 2.0 * ub[0, r, :] - dot(tb[1, r, :], tb[1])
            ub[1, r, :] = v
            tb[2, r, :] = v.astype(bf16)
        for r in halves:
            y = twice * full[r, :] + 2.0 * ub[0, r, :] - dot(tb[0, r, :], tb[1])
            last = 4.0 * ub[1, r, :] + 2.0 * y - dot(y.astype(bf16), tb[2])
            dst[r, :] = last.astype(bf16)

    last = 2 * STAGES
    early = ahead >= STAGES

    def both(t, carry):
        b_stage(t, True)

        @pl.when(ahead + t <= last)
        def _():
            a_stage(ahead + t)

        @pl.when(jnp.logical_and(early, t == last - 2))
        def _():
            for k in range(len(a_pieces)):
                a_finish(k)
            newton(a_red, 0, za_ref)

        return carry

    lax.fori_loop(0, last + 1, both, 0)

    @pl.when(jnp.logical_not(early))
    def _():
        for k in range(len(a_pieces)):
            a_finish(k)
        newton(a_red, 0, za_ref)

    dx_copy.wait_recv()
    put_mine.start()
    put_theirs.start()
    def left(r, carry):
        dh_copy(r).wait_send()
        return carry

    lax.fori_loop(0, rows // ROWS, left, 0)

    @pl.when(chip > 0)
    def _():
        def left(r, carry):
            chain_copy(r).wait_send()
            return carry

        lax.fori_loop(0, rows // ROWS, left, 0)

    a_drain()
    b_drain()
    x_copy.wait_send()
    w_copy.wait_send()
    dx_copy.wait_send()

    b_finish(0)
    newton(b_red, 1, zb)
    b_finish(1)
    scale = inv[0, 0:1, 0:1] * inv[1, 0:1, 0:1]
    for r in halves:
        strips = []
        for i in range(r.start // T, r.stop // T):
            blocks = [tri + (i * nb + j) * T for j in range(nb)]
            strips.append(jnp.concatenate([b_red[at:at + T, :] for at in blocks], axis=1))
        g = jnp.concatenate(strips, axis=0)
        h_ref[r, :] = (8.0 * g.astype(f32) - dot(g, zb[...])) * scale

    put_mine.wait()
    put_theirs.wait()


def finish_kernel(dx_ref, h_ref, za_ref, dx_hbm, up_hbm, up, sem):
    put_dx = pltpu.make_async_copy(dx_ref, dx_hbm, sem.at[0])
    put_dx.start()
    h = h_ref[...].astype(jnp.bfloat16)
    puts = []
    for i in range(up.shape[0] // T):
        r = slice(i * T, (i + 1) * T)
        up[r, :] = 8.0 * h_ref[r, :] - dot(za_ref[r, :], h)
        put = pltpu.make_async_copy(up.at[r, :], up_hbm.at[0, r, :], sem.at[1 + i])
        put.start()
        puts.append(put)
    put_dx.wait()
    for put in puts:
        put.wait()


def body(rings, acts, weights, cot_last):
    sections = lax.axis_size("section")
    size = lax.axis_size("dp") // rings
    _, micro, rows, width = acts.shape
    vmem = pl.BlockSpec(memory_space=pltpu.VMEM)
    hbm = pl.BlockSpec(memory_space=pltpu.HBM)
    bf16, f32 = jnp.bfloat16, jnp.float32
    dma = pltpu.SemaphoreType.DMA

    def ring_scratch(pieces):
        piece = sum(n for n, _, _ in pieces)
        passing = pltpu.VMEM((2, STAGES, piece, T), bf16)
        whole = pltpu.VMEM((piece * size, T), bf16)
        message = pltpu.VMEM((piece, T), bf16)
        return [whole, passing, passing, passing, whole, message, message]

    a_pieces, b_pieces = ring_of(width, size)
    dx, h, za = pl.pallas_call(
        functools.partial(kernel, sections, rings, size),
        name="relay",
        out_shape=(
            jax.ShapeDtypeStruct((1, micro, rows, width), bf16),
            jax.ShapeDtypeStruct((width, width), f32),
            jax.ShapeDtypeStruct((width, width), bf16),
        ),
        in_specs=[hbm] * 3,
        out_specs=(vmem, vmem, vmem),
        scratch_shapes=[
            pltpu.VMEM((micro, rows, width), bf16),
            pltpu.VMEM((2, width, width), bf16),
            pltpu.VMEM((2, width, width), bf16),
            pltpu.VMEM((rows, width), bf16),
            pltpu.VMEM((2, rows, width), f32),
            pltpu.VMEM((width, micro * rows), bf16),
            pltpu.VMEM((rows, width), bf16),
            pltpu.VMEM((2, rows, width), bf16),
            pltpu.VMEM((2, rows, width), bf16),
            pltpu.VMEM((rows, width), bf16),
            pltpu.VMEM((rows, width), bf16),
            *ring_scratch(a_pieces),
            *ring_scratch(b_pieces),
            pltpu.VMEM((width, width), f32),
            pltpu.VMEM((3, width, width), bf16),
            pltpu.VMEM((2, width, width), f32),
            pltpu.VMEM((width, width), bf16),
            pltpu.VMEM((2, 8, T), f32),
            dma((5,)), dma((2, 3)),
            dma((rows // ROWS,)), dma((rows // ROWS,)),
            dma((rows // ROWS,)), dma((rows // ROWS,)),
            dma((2, 4, 2, STAGES, len(a_pieces))), dma((2, len(a_pieces))),
            dma((2, 4, 2, STAGES, len(b_pieces))), dma((2, len(b_pieces))),
        ],
        compiler_params=pltpu.CompilerParams(
            collective_id=0, has_side_effects=True, vmem_limit_bytes=48 << 20
        ),
    )(*(pltpu.with_memory_space_constraint(a, pltpu.HBM) for a in (acts, weights, cot_last)))
    return pl.pallas_call(
        finish_kernel,
        name="finish",
        out_shape=(
            jax.ShapeDtypeStruct((1, micro, rows, width), bf16),
            jax.ShapeDtypeStruct((1, width, width), f32),
        ),
        in_specs=[vmem] * 3,
        out_specs=(hbm, hbm),
        scratch_shapes=[
            pltpu.VMEM((width, width), f32),
            dma((1 + width // T,)),
        ],
        compiler_params=pltpu.CompilerParams(vmem_limit_bytes=8 << 20),
    )(dx, h, za)


def solution(mesh):
    placed = (P("section", None, "dp", None), P("section", None, None), P(None, "dp", None))
    return jax.shard_map(
        functools.partial(body, 2),
        mesh=mesh,
        in_specs=placed,
        out_specs=(P("section", None, "dp", None), P("section", None, None)),
        check_vma=False,
    )
```
